32 devices in a mesh: draws: 2 (over x), spec: 16 (over z, y, core).
Axes of the slice: x: 2, y: 2, z: 4, core: 2. Of those that a mesh axis runs over, the one named last changes fastest.
Arguments:
- coefficients: bfloat16 [1280, 2, 320, 128], P('draws', None, 'spec'), parts along dimension 0, may hold values from -6 to 6
- legendre: float32 [640, 2, 320, 16], P('spec'), as said below
- row_counts: int32 [16], P('spec'), may hold values from 640 to 1280, as said below
- basis: float32 [64, 128], replicated, may hold values from -0.75 to 0.75
- absorb: float32 [128], replicated, may hold values from 0.00390625 to 0.0625
- peak_level: int32 [512], replicated, may hold values from 0 to 127
- width: float32 [512], replicated, may hold values from 1.5 to 12
Outputs:
- radiance: float32 [32, 2, 1280, 512], P(('draws', 'spec')), parts along dimension 0
The draws below stay inside these ranges and needn't reach their ends.
There are 2 independent parts, one for each index of `draws`. The reference program is written for one: setup_inputs(seed, part) draws one part's arguments, and reference() takes and returns one part's arrays. A program takes and returns all parts, laid end to end along the dimension named above; an argument that names none is the same for every part. Nothing has to cross between parts.
Inputs may be any that keep to these rules, and one draw needn't show every extreme that they name: `legendre`: entry [m, p, s, j] is the associated Legendre function of order m and degree m + 2 s + p, normalised to unit square integral over [-1, 1], at the cosine of a drawn colatitude of row j in the northern hemisphere; it is zero where the degree exceeds 640 - 1. `row_counts`: every count is a multiple of 4; row 0 has 1280 longitudes and row 1 has 640.
All inputs are finite; a program needn't handle non-finite values.
Results may differ from the reference program's by a relative error of at most 0.0003.
Values sent between devices are 32-bit elements; how exact they have to be, the bound alone decides.
A program may use at most 128 MiB of HBM per device.

```python
import math
import jax
import jax.numpy as jnp
from jax import lax

MW = 640
NE = 320
NLON = 1280
NCH = 512
LEV = 128
K = 64
PR = 16


def draw_legendre(key, part):
    jitter = jax.random.uniform(key, (PR,), jnp.float32)
    colatitude = 0.5 * math.pi * (jnp.arange(PR, dtype=jnp.float32) + 0.2 + 0.6 * jitter) / PR
    cosine = jnp.cos(colatitude)
    log_sine = jnp.log(jnp.sin(colatitude))
    orders = jnp.arange(MW, dtype=jnp.float32)
    growth = jnp.concatenate((jnp.zeros((1,), jnp.float32), 0.5 * jnp.log((2.0 * orders[1:] + 1.0) / (2.0 * orders[1:]))))
    log_start = 0.5 * math.log(0.5) + jnp.cumsum(growth)
    diagonal_start = jnp.exp(log_start[:, None] + orders[:, None] * log_sine[None, :])

    def advance(carry, offset):
        previous, current = carry
        degree = orders + offset
        below = degree - 1.0
        coupling_now = jnp.sqrt(jnp.maximum((degree * degree - orders * orders) / (4.0 * degree * degree - 1.0), 0.0))
        coupling_prev = jnp.sqrt(jnp.maximum((below * below - orders * orders) / (4.0 * below * below - 1.0), 0.0))
        following = (cosine[None, :] * current - coupling_prev[:, None] * previous) / coupling_now[:, None]
        return ((current, following), following)
    offsets = jnp.arange(1, MW, dtype=jnp.float32)
    carried, values = lax.scan(advance, (jnp.zeros_like(diagonal_start), diagonal_start), offsets)
    whole = jnp.concatenate((diagonal_start[None], values), axis=0)
    degree_offset = jnp.arange(MW, dtype=jnp.int32)[:, None, None]
    order_index = jnp.arange(MW, dtype=jnp.int32)[None, :, None]
    whole = jnp.where(degree_offset + order_index < MW, whole, jnp.zeros_like(whole))
    arranged = whole.reshape(MW // 2, 2, MW, PR)
    return jnp.transpose(arranged, (2, 1, 0, 3)).astype(jnp.float32)


def draw_row_counts(key, part):
    increments = jax.random.randint(key, (PR,), 0, NLON // 8 + 1)
    counts = NLON // 2 + 4 * increments
    counts = counts.at[0].set(NLON).at[1].set(NLON // 2)
    return counts.astype(jnp.int32)


def set_ends(values, rng, low, high):
    index_at = [jax.random.randint(jax.random.fold_in(rng, axis), (), 0, length) for axis, length in enumerate(values.shape)]
    main_axis = values.shape.index(max(values.shape))
    next_to = index_at[:main_axis] + [(index_at[main_axis] + 1) % values.shape[main_axis]] + index_at[main_axis + 1:]
    return values.at[tuple(index_at)].set(low).at[tuple(next_to)].set(high)


def shard_levels(own_key, extent, cuts, smallest, top_value):
    gain, own = 1.0, jax.random.fold_in(own_key, 6)
    for position, parts in cuts:
        draws = jnp.exp(jax.random.uniform(jax.random.fold_in(own, position), (parts,), jnp.float32, smallest / len(cuts), top_value / len(cuts)))
        gain = gain * jnp.repeat(draws, extent[position] // parts).reshape([-1 if axis == position else 1 for axis in range(len(extent))])
    return gain


def centred(own_key, extent, scale, most, cuts=(), kind=jnp.bfloat16):
    entries = scale * jax.random.normal(own_key, extent, jnp.float32)
    if cuts:
        entries = entries * shard_levels(own_key, extent, cuts, -0.22, 0.18)
    return jnp.clip(entries, -most, most).astype(kind)


def setup_inputs(seed: int = 0, part: int = 0) -> dict:
    streams_of = jax.random.split(jax.random.key(seed), 8)
    part_splits = jax.random.split(jax.random.fold_in(streams_of[7], part), 8)
    coefficients = centred(part_splits[0], (MW, 2, NE, 2 * K), 1.0, 6.0, ((2, 16),))
    legendre = draw_legendre(jax.random.fold_in(streams_of[7], 71), part)
    row_counts = draw_row_counts(jax.random.fold_in(streams_of[7], 71), part)
    basis = centred(streams_of[3], (K, LEV), K ** -0.5, 0.75, (), jnp.float32)
    absorb = jnp.clip(jnp.exp(jax.random.uniform(streams_of[4], (LEV,), jnp.float32, math.log(0.00390625), math.log(0.0625))), 0.00390625, 0.0625)
    peak_level = set_ends(jax.random.randint(streams_of[5], (NCH,), 0, LEV), jax.random.fold_in(streams_of[5], 1), 0, LEV - 1).astype(jnp.int32)
    width = jnp.clip(jnp.exp(jax.random.uniform(streams_of[6], (NCH,), jnp.float32, math.log(1.5), math.log(12.0))), 1.5, 12.0)
    return {"coefficients": coefficients, "legendre": legendre, "row_counts": row_counts, "basis": basis, "absorb": absorb, "peak_level": peak_level, "width": width}


PRECISE = lax.Precision.HIGHEST

def prior_scale(shard, first):
    waves = shard.shape[0]
    slots = shard.shape[2]
    orders = jnp.arange(waves, dtype=jnp.int32)[:, None, None]
    parity = jnp.arange(2, dtype=jnp.int32)[None, :, None]
    slot_index = first + jnp.arange(slots, dtype=jnp.int32)[None, None, :]
    degree = orders + 2 * slot_index + parity
    spread = lax.rsqrt((degree + 1).astype(jnp.float32) * waves)
    spread = jnp.where(degree < waves, spread, jnp.zeros_like(spread))
    return shard.astype(jnp.float32) * spread[..., None]

def expand_levels(values, modes_basis):
    lead = values.shape[:-1]
    halves = values.reshape(lead + (2, modes_basis.shape[0]))
    expanded = jnp.einsum('abcqk,kl->abcql', halves, modes_basis, precision=PRECISE)
    return expanded.reshape(lead + (2 * modes_basis.shape[1],))

def channel_kernel(peak_level, width, levels):
    height = jnp.arange(levels, dtype=jnp.float32)[:, None]
    offsets = (height - peak_level.astype(jnp.float32)[None, :]) / width[None, :]
    weights = jnp.exp(-offsets * offsets)
    return weights / lax.optimization_barrier(jnp.sum(weights, axis=0, keepdims=True))

def radiate(temps, absorb, kernel):
    levels = temps.shape[-1]
    strict_upper = (jnp.arange(levels)[:, None] < jnp.arange(levels)[None, :]).astype(jnp.float32)
    source = jnp.exp(0.5 * temps)
    layers = absorb[None, :] * source
    overhead = jnp.dot(layers, strict_upper, precision=PRECISE, preferred_element_type=jnp.float32)
    emitted = source * jnp.exp(-overhead) * -jnp.expm1(-layers)
    return jnp.dot(emitted, kernel, precision=PRECISE, preferred_element_type=jnp.float32)

def fourier_lookup(row_count, waves, points):
    orders = jnp.arange(waves, dtype=jnp.int32)
    places = jnp.arange(points, dtype=jnp.int32)
    phases = places[:, None] * orders[None, :] % row_count
    angles = 2.0 * math.pi * phases.astype(jnp.float32) / row_count.astype(jnp.float32)
    weights = jnp.where(orders == 0, 1.0, 2.0) * (2 * orders < row_count).astype(jnp.float32)
    return jnp.stack((weights * jnp.cos(angles), -weights * jnp.sin(angles)), axis=-1)

def synthesize_row(spectra, row_count, modes_basis, absorb, kernel, points):
    waves, hemis, columns = spectra.shape
    lookup = fourier_lookup(row_count, waves, points)
    split_parts = spectra.reshape(waves, hemis, 2, columns // 2)
    fields = jnp.einsum('kmq,mhqc->hkc', lookup, split_parts, precision=PRECISE)
    if modes_basis is not None:
        fields = jnp.einsum('hkc,cl->hkl', fields, modes_basis, precision=PRECISE)
    levels = fields.shape[-1]
    bright = radiate(fields.reshape(hemis * points, levels), absorb, kernel)
    bright = bright.reshape(hemis, points, kernel.shape[1])
    inside = (jnp.arange(points, dtype=jnp.int32) < row_count).astype(jnp.float32)
    return bright * inside[None, :, None]

def reference(coefficients, legendre, row_counts, basis, absorb, peak_level, width):
    scaled = prior_scale(coefficients, 0)
    spectral = expand_levels(scaled, basis)
    even_odd = jnp.einsum('mpsj,mpsc->mpjc', legendre, spectral, precision=PRECISE)
    fourier = jnp.stack((even_odd[:, 0] + even_odd[:, 1], even_odd[:, 0] - even_odd[:, 1]), axis=1)
    kernel = channel_kernel(peak_level, width, LEV)

    def one_row(inputs):
        spectra, row_count = inputs
        return synthesize_row(spectra, row_count, None, absorb, kernel, NLON)
    return lax.map(one_row, (jnp.moveaxis(fourier, 2, 0), row_counts))
```

```python
import math

import jax
import jax.numpy as jnp
from jax import lax
from jax.experimental import pallas as pl
from jax.experimental.pallas import tpu as pltpu
from jax.sharding import PartitionSpec as P

NLON = 1280
FINE = 128

PRECISE = lax.Precision.HIGHEST
F32 = jnp.float32
BF16 = jnp.bfloat16


def prior_spread(orders, slots, waves):
    parity = jnp.arange(2, dtype=jnp.int32)[None, :, None]
    degree = orders[:, None, None] + 2 * slots[None, None, :] + parity
    spread = lax.rsqrt((degree + 1).astype(F32) * waves)
    return jnp.where(degree < waves, spread, jnp.zeros_like(spread))


def channel_kernel(peak_level, width, levels):
    height = jnp.arange(levels, dtype=F32)[:, None]
    offsets = (height - peak_level.astype(F32)[None, :]) / width[None, :]
    weights = jnp.exp(-offsets * offsets)
    return weights / jnp.sum(weights, axis=0, keepdims=True)


def split(x):
    high = x.astype(BF16)
    return high, (x - high.astype(F32)).astype(BF16)


def dot(a, b):
    return jnp.dot(a, b, preferred_element_type=F32)


def dot3(a, b):
    ah, al = split(a)
    bh, bl = split(b)
    return dot(ah, bh) + dot(al, bh) + dot(ah, bl)


def partial_kernel(pairs, padded, coef_ref, leg_ref, out_ref, pad_ref):
    waves, parities, slots, columns = coef_ref.shape
    groups = leg_ref.shape[0]
    per = pairs // 2
    lanes = leg_ref.shape[2]
    rows = lanes // pairs
    pad_ref[...] = jnp.zeros_like(pad_ref)
    owner = lax.broadcasted_iota(jnp.int32, (pairs, padded, lanes), 0)
    lane = lax.broadcasted_iota(jnp.int32, (pairs, padded, lanes), 2)
    keep = (lane % pairs == owner).reshape(pairs * padded, lanes)

    for g in range(groups):
        for i in range(pairs):
            pad_ref[g, i, pl.ds(0, slots), :] = coef_ref[g * per + i // 2, i % 2].astype(F32)
        values = pad_ref[g].reshape(pairs * padded, columns).astype(BF16)
        legs = leg_ref[g]
        if padded > slots:
            legs = jnp.concatenate((legs, jnp.zeros((padded - slots, lanes), F32)), axis=0)
        tiled = jnp.where(keep, jnp.concatenate([legs] * pairs, axis=0), 0.0)
        high, low = split(tiled)
        both = jnp.concatenate((high, low), axis=1)
        sums = lax.dot_general(both, values, (((0,), (0,)), ((), ())), preferred_element_type=F32)
        sums = sums[:lanes] + sums[lanes:]
        out_ref[:, pl.ds(g * pairs, pairs), :] = sums.reshape(rows, pairs, columns)


def partial_sums(coefficients, legs, pairs):
    waves, parities, slots, columns = coefficients.shape
    groups, _, lanes = legs.shape
    rows = lanes // pairs
    per = pairs // 2
    block = next(b for b in (8, 5, 4, 2, 1) if groups % b == 0)
    padded = -(-slots // 8) * 8
    if (pairs * padded) % 16:
        padded += 8

    def body(*refs):
        partial_kernel(pairs, padded, *refs)

    return pl.pallas_call(
        body,
        out_shape=jax.ShapeDtypeStruct((rows, groups * pairs, columns), F32),
        grid=(groups // block,),
        in_specs=[
            pl.BlockSpec((block * per, parities, slots, columns), lambda i: (i, 0, 0, 0)),
            pl.BlockSpec((block, slots, lanes), lambda i: (i, 0, 0)),
        ],
        out_specs=pl.BlockSpec((rows, block * pairs, columns), lambda i: (0, i, 0)),
        scratch_shapes=[pltpu.VMEM((block, pairs, padded, columns), F32)],
        name="partial_sums",
    )(coefficients, legs)


def row_kernel(
    count_ref, spectra_ref, fcos_ref, fsin_ref, ccos_ref, csin_ref, wide_ref, absorb_ref, resp_ref, out_ref,
    high_ref, low_ref, rhigh_ref, rlow_ref,
):
    step = pl.program_id(0)
    waves = fcos_ref.shape[1]
    levels = absorb_ref.shape[1]
    points = fcos_ref.shape[0]

    @pl.when(step == 0)
    def _():
        even = spectra_ref[pl.ds(0, waves, stride=2), :]
        odd = spectra_ref[pl.ds(1, waves, stride=2), :]
        half = even.shape[1] // 2
        real = jnp.concatenate((even[:, :half], odd[:, :half]), axis=1)
        imag = jnp.concatenate((even[:, half:], odd[:, half:]), axis=1)
        wide = wide_ref[...]
        for index, piece in enumerate((real, imag)):
            high, low = split(dot3(piece, wide))
            high_ref[pl.ds(index * waves, waves), :] = high
            low_ref[pl.ds(index * waves, waves), :] = low
        high, low = split(resp_ref[...])
        rhigh_ref[pl.ds(0, levels), :] = high
        rhigh_ref[pl.ds(levels, levels), :] = high
        rlow_ref[...] = low

    base_c = ccos_ref[pl.ds(step, 1), :]
    base_s = csin_ref[pl.ds(step, 1), :]
    fine_c = fcos_ref[...]
    fine_s = fsin_ref[...]
    cosine = base_c * fine_c - base_s * fine_s
    sine = -(base_s * fine_c + base_c * fine_s)
    lookup_high, lookup_low = split(jnp.concatenate((cosine, sine), axis=1))
    high = high_ref[...]
    temps = dot(lookup_high, high) + dot(lookup_low, high) + dot(lookup_high, low_ref[...])
    temps = jnp.concatenate((temps[:, :levels], temps[:, levels:]), axis=0)

    source = jnp.exp(0.5 * temps)
    layers = absorb_ref[...] * source
    before = lax.broadcasted_iota(jnp.int32, (2 * levels, levels), 0) % levels
    after = lax.broadcasted_iota(jnp.int32, (2 * levels, levels), 1)
    upper = jnp.where(before < after, 1.0, 0.0).astype(BF16)
    layers_high, layers_low = split(layers)
    above = dot(jnp.concatenate((layers_high, layers_low), axis=1), upper)
    emitted = source * jnp.exp(-above) * (1.0 - jnp.exp(-layers))
    place = step * points + lax.broadcasted_iota(jnp.int32, (2 * points, levels), 0) % points
    emitted = jnp.where(place < count_ref[0], emitted, 0.0)
    emitted_high, emitted_low = split(emitted)
    bright = dot(jnp.concatenate((emitted_high, emitted_low), axis=1), rhigh_ref[...])
    bright = bright + dot(emitted_high, rlow_ref[...])
    out_ref[0, 0] = bright[:points]
    out_ref[0, 1] = bright[points:]


def row_tables(row_count, waves, points):
    orders = jnp.arange(waves, dtype=jnp.int32)

    def angles(places):
        phases = places[:, None] * orders[None, :] % row_count
        return 2.0 * math.pi * phases.astype(F32) / row_count.astype(F32)

    fine = angles(jnp.arange(FINE, dtype=jnp.int32))
    coarse = angles(FINE * jnp.arange(points // FINE, dtype=jnp.int32))
    weights = jnp.where(orders == 0, 1.0, 2.0) * (2 * orders < row_count).astype(F32)
    return jnp.cos(fine), jnp.sin(fine), weights * jnp.cos(coarse), weights * jnp.sin(coarse)


def synthesize_row(spectra, row_counts, basis, absorb, kernel, points):
    waves = spectra.shape[0] // 2
    levels, channels = kernel.shape
    columns = spectra.shape[1]
    fcos, fsin, ccos, csin = row_tables(row_counts[0], waves, points)
    top = jnp.concatenate((basis, basis), axis=1)
    wide = jnp.concatenate((top, jnp.concatenate((basis, -basis), axis=1)), axis=0)
    steps = points // FINE

    def whole(*shape):
        return pl.BlockSpec(shape, lambda i, *_: (0,) * len(shape))

    return pl.pallas_call(
        row_kernel,
        out_shape=jax.ShapeDtypeStruct((1, 2, points, channels), F32),
        grid_spec=pltpu.PrefetchScalarGridSpec(
            num_scalar_prefetch=1,
            grid=(steps,),
            in_specs=[
                whole(2 * waves, columns),
                whole(FINE, waves),
                whole(FINE, waves),
                whole(steps, waves),
                whole(steps, waves),
                whole(*wide.shape),
                whole(1, levels),
                whole(levels, channels),
            ],
            out_specs=pl.BlockSpec((1, 2, FINE, channels), lambda i, *_: (0, 0, i, 0)),
            scratch_shapes=[
                pltpu.VMEM((2 * waves, 2 * levels), BF16),
                pltpu.VMEM((2 * waves, 2 * levels), BF16),
                pltpu.VMEM((2 * levels, channels), BF16),
                pltpu.VMEM((levels, channels), BF16),
            ],
        ),
        name="row_synthesis",
    )(row_counts, spectra, fcos, fsin, ccos, csin, wide, absorb[None, :], kernel)


def moved_coefficients(coefficients, legendre):
    waves, _, slots, _ = coefficients.shape
    first = lax.axis_index("spec") * slots
    spread = prior_spread(jnp.arange(waves, dtype=jnp.int32), first + jnp.arange(slots, dtype=jnp.int32), waves)
    scaled = coefficients.astype(F32) * spread[..., None]
    spectral = lax.all_to_all(scaled, "spec", split_axis=0, concat_axis=2, tiled=True)
    sums = jnp.einsum("mpsj,mpsc->mpjc", legendre, spectral, precision=PRECISE)
    sums = lax.all_to_all(sums, "spec", split_axis=2, concat_axis=0, tiled=True)
    return sums.reshape(2 * waves, sums.shape[-1])


def moved_legendre(coefficients, legendre, pairs):
    waves, _, slots, columns = coefficients.shape
    own, _, every, rows = legendre.shape
    orders = lax.axis_index("spec") * own + jnp.arange(own, dtype=jnp.int32)
    spread = prior_spread(orders, jnp.arange(every, dtype=jnp.int32), waves)
    legs = (legendre * spread[..., None]).reshape(own * 2 // pairs, pairs // 2, 2, every, rows)
    legs = jnp.transpose(legs, (0, 3, 4, 1, 2)).reshape(own * 2 // pairs, every, rows * pairs)
    legs = lax.all_to_all(legs, "spec", split_axis=1, concat_axis=0, tiled=True)
    sums = partial_sums(coefficients, legs, pairs)
    sums = lax.psum_scatter(sums, "spec", scatter_dimension=0, tiled=True)
    return sums.reshape(2 * waves, columns)


def on_device(coefficients, legendre, row_counts, basis, absorb, peak_level, width):
    kernel = channel_kernel(peak_level, width, basis.shape[1])
    own, _, _, rows = legendre.shape
    pairs = 128 // rows
    if pairs % 8 == 0 and (2 * own) % pairs == 0:
        spectra = moved_legendre(coefficients, legendre, pairs)
    else:
        spectra = moved_coefficients(coefficients, legendre)
    return synthesize_row(spectra, row_counts, basis, absorb, kernel, NLON)


def solution(mesh):
    placed = (
        P("draws", None, "spec", None),
        P("spec", None, None, None),
        P("spec"),
        P(),
        P(),
        P(),
        P(),
    )
    return jax.shard_map(
        on_device,
        mesh=mesh,
        in_specs=placed,
        out_specs=P(("draws", "spec"), None, None, None),
        check_vma=False,
    )
```

```python
import math

import jax
import jax.numpy as jnp
from jax import lax
from jax.experimental import pallas as pl
from jax.experimental.pallas import tpu as pltpu
from jax.sharding import PartitionSpec as P

NLON = 1280
FINE = 128

PRECISE = lax.Precision.HIGHEST
F32 = jnp.float32
BF16 = jnp.bfloat16


def prior_spread(orders, slots, waves):
    parity = jnp.arange(2, dtype=jnp.int32)[None, :, None]
    degree = orders[:, None, None] + 2 * slots[None, None, :] + parity
    spread = lax.rsqrt((degree + 1).astype(F32) * waves)
    return jnp.where(degree < waves, spread, jnp.zeros_like(spread))


def channel_kernel(peak_level, width, levels):
    height = jnp.arange(levels, dtype=F32)[:, None]
    offsets = (height - peak_level.astype(F32)[None, :]) / width[None, :]
    weights = jnp.exp(-offsets * offsets)
    return weights / jnp.sum(weights, axis=0, keepdims=True)


def split(x):
    high = x.astype(BF16)
    return high, (x - high.astype(F32)).astype(BF16)


def dot(a, b):
    return jnp.dot(a, b, preferred_element_type=F32)


def dot3(a, b):
    ah, al = split(a)
    bh, bl = split(b)
    return dot(ah, bh) + dot(al, bh) + dot(ah, bl)


def place_in_ring(n):
    me = lax.axis_index("spec")
    core = me % 2
    side = (me // 2) % 2
    layer = me // 4
    return me, core, side, layer


def exchange_kernel(
    n, waves, coef_ref, leg_ref, out_ref, send_ref, legs_ref, wide_ref, sums_ref, near_ref, side_ref, far_ref,
    leg_send, leg_recv, near_send, near_recv, side_send, side_recv, far_send, far_recv,
):
    me, core, side, layer = place_in_ring(n)
    layers = n // 4
    chunks = n // 2
    chip = me // 2
    rows = n
    columns = coef_ref.shape[1]
    every = leg_ref.shape[1]
    slots = every // n
    lanes = 128
    pairs = lanes // rows
    per = pairs // 2
    own = waves // n
    groups = own // per
    depth = per * slots * 2
    part = groups * pairs
    partner = me + 1 - 2 * core
    across = me + 2 - 4 * side

    def spot(z, y, c):
        return (z * 2 + y) * 2 + c

    def remote(src, dst, send_sem, recv_sem, target):
        return pltpu.make_async_remote_copy(
            src_ref=src, dst_ref=dst, send_sem=send_sem, recv_sem=recv_sem,
            device_id={"spec": target}, device_id_type=pl.DeviceIdType.MESH,
        )

    def leg_copy(source, target):
        return remote(send_ref.at[target], legs_ref.at[source], leg_send.at[target], leg_recv.at[source], target)

    def near_copy(q):
        return remote(sums_ref.at[q, 1 - core], near_ref.at[q], near_send.at[q], near_recv.at[q], partner)

    def side_copy(q):
        return remote(sums_ref.at[q, core, 1 - side], side_ref.at[q], side_send.at[q], side_recv.at[q], across)

    def far_copy(q, source, target):
        return remote(
            sums_ref.at[q, core, side, target], far_ref.at[source, q],
            far_send.at[target, q], far_recv.at[source, q], spot(target, side, core),
        )

    others = [(dz, dy, dc) for dz in range(layers) for dy in range(2) for dc in range(2)][1:]

    def other(offset):
        dz, dy, dc = offset
        return spot((layer + dz) % layers, (side + dy) % 2, (core + dc) % 2)

    barrier = pltpu.get_barrier_semaphore()
    for offset in others:
        pl.semaphore_signal(barrier, inc=1, device_id={"spec": other(offset)}, device_id_type=pl.DeviceIdType.MESH)

    row = lax.broadcasted_iota(jnp.int32, (lanes, lanes), 0)
    lane = lax.broadcasted_iota(jnp.int32, (lanes, lanes), 1)
    row_at = row % rows
    ordered = ((row_at % 2) * 2 + (row_at // 2) % 2) * layers + row_at // 4
    moves = jnp.where(ordered * pairs + row // rows == lane, 1.0, 0.0)
    leg_row = lax.broadcasted_iota(jnp.int32, (lanes, every), 0) // rows
    leg_slot = lax.broadcasted_iota(jnp.int32, (lanes, every), 1)
    degree_part = leg_row // 2 + leg_row % 2 + 2 * leg_slot

    @pl.loop(0, groups // 2)
    def _(double):
        turned = []
        for half in range(2):
            g = double * 2 + half
            degree = degree_part + (me * own + g * per)
            spread = lax.rsqrt((degree + 1).astype(F32) * float(waves))
            spread = jnp.where(degree < waves, spread, 0.0)
            values = leg_ref[pl.ds(pl.multiple_of(g * lanes, lanes), lanes), :] * spread
            turned.append(
                lax.dot_general(
                    values, moves, (((0,), (0,)), ((), ())), precision=PRECISE, preferred_element_type=F32
                )
            )
        for k in range(n):
            piece = [t[k * slots:(k + 1) * slots] for t in turned]
            send_ref[k, pl.ds(pl.multiple_of(double * 2 * slots, 2 * slots), 2 * slots), :] = jnp.concatenate(piece, 0)

    pl.semaphore_wait(barrier, len(others))
    for offset in others:
        target = other(offset)

        @pl.when(me + target < n)
        def _():
            leg_copy(me, target).start()

    legs_ref[me] = send_ref[me]

    expand_row = lax.broadcasted_iota(jnp.int32, (depth, lanes), 0)
    expand_lane = lax.broadcasted_iota(jnp.int32, (depth, lanes), 1) % pairs
    keep = (expand_row // (2 * slots)) * 2 + expand_row % 2 == expand_lane

    def partial(q, which):
        owner = 2 * q + which

        @pl.when(me + owner < n)
        def _():
            @pl.when(owner != me)
            def _():
                leg_copy(owner, me).wait_recv()

            @pl.loop(0, groups // 2)
            def _(double):
                legs = legs_ref[owner, pl.ds(pl.multiple_of(double * 2 * slots, 2 * slots), 2 * slots), :]
                wide_ref[pl.ds(0, 2 * slots, stride=2), :] = legs
                wide_ref[pl.ds(1, 2 * slots, stride=2), :] = legs
                for half in range(2):
                    g = owner * groups + double * 2 + half
                    values = coef_ref[pl.ds(pl.multiple_of(g * depth, depth), depth), :]
                    one = wide_ref[pl.ds(half * 2 * slots, 2 * slots), :]
                    tiled = jnp.where(keep, jnp.concatenate([one] * per, axis=0), 0.0)
                    both = jnp.concatenate(split(tiled), axis=1)
                    sums = lax.dot_general(both, values, (((0,), (0,)), ((), ())), preferred_element_type=F32)
                    sums = (sums[:lanes] + sums[lanes:]).reshape(2, 2, layers, pairs, columns)
                    at = pl.multiple_of(which * part + (double * 2 + half) * pairs, pairs)
                    sums_ref[q, :, :, :, pl.ds(at, pairs), :] = sums

        @pl.when(me + owner >= n)
        def _():
            sums_ref[q, :, :, :, pl.ds(which * part, part), :] = jnp.zeros((2, 2, layers, part, columns), F32)

    def compute(q):
        @pl.when(q + chip < chunks)
        def _():
            partial(q, 0)
            partial(q, 1)
            near_copy(q).start()

    def merge_near(q):
        @pl.when(q + chip < chunks)
        def _():
            near_copy(q).wait_recv()

            for y in (0, 1):
                @pl.loop(0, layers)
                def _(z):
                    sums_ref[q, core, y, z] += near_ref[q, y, z]

            side_copy(q).start()

    def merge_side(q):
        here = q + chip < chunks
        there = q + across // 2 < chunks

        @pl.when(there)
        def _():
            side_copy(q).wait_recv()

        @pl.when(jnp.logical_and(here, there))
        def _():
            @pl.loop(0, layers)
            def _(z):
                sums_ref[q, core, side, z] += side_ref[q, z]

        @pl.when(jnp.logical_and(jnp.logical_not(here), there))
        def _():
            @pl.loop(0, layers)
            def _(z):
                sums_ref[q, core, side, z] = side_ref[q, z]

        @pl.when(jnp.logical_or(here, there))
        def _():
            for dz in range(1, layers):
                far_copy(q, layer, (layer + dz) % layers).start()

    lag = min(5, chunks)

    @pl.loop(0, chunks + 1)
    def _(t):
        @pl.when(t < chunks)
        def _():
            compute(t)

        @pl.when(t >= 1)
        def _():
            merge_near(t - 1)

        @pl.when(t >= lag)
        def _():
            merge_side(t - lag)

    @pl.loop(chunks + 1 - lag, chunks)
    def _(q):
        merge_side(q)

    @pl.loop(0, chunks)
    def _(q):
        at = pl.ds(pl.multiple_of(q * 2 * part, 2 * part), 2 * part)

        @pl.when(q + 2 * layer < chunks)
        def _():
            out_ref[at, :] = sums_ref[q, core, side, layer]

        @pl.when(q + 2 * layer >= chunks)
        def _():
            out_ref[at, :] = jnp.zeros((2 * part, columns), F32)

        for dz in range(1, layers):
            source = (layer + dz) % layers

            @pl.when(q + 2 * source < chunks)
            def _():
                far_copy(q, source, layer).wait_recv()
                out_ref[at, :] += far_ref[source, q]

    for offset in others:
        target = other(offset)

        @pl.when(me + target < n)
        def _():
            leg_copy(me, target).wait_send()

    @pl.loop(0, chunks)
    def _(q):
        @pl.when(q + chip < chunks)
        def _():
            near_copy(q).wait_send()
            side_copy(q).wait_send()

        @pl.when(q + 2 * layer < chunks)
        def _():
            for dz in range(1, layers):
                far_copy(q, layer, (layer + dz) % layers).wait_send()


def exchanged_sums(coefficients, legendre, n):
    waves, _, slots, columns = coefficients.shape
    own, _, every, rows = legendre.shape
    dense = jnp.transpose(coefficients, (0, 2, 1, 3)).reshape(waves * slots * 2, columns)
    legs = jnp.transpose(legendre, (0, 1, 3, 2)).reshape(own * 2 * rows, every)
    layers, chunks = n // 4, n // 2
    pairs = 128 // rows
    groups = own * 2 // pairs
    width = 2 * groups * pairs
    dma = pltpu.SemaphoreType.DMA

    def body(*refs):
        exchange_kernel(n, waves, *refs)

    return pl.pallas_call(
        body,
        out_shape=jax.ShapeDtypeStruct((2 * waves, columns), F32),
        in_specs=[pl.BlockSpec(memory_space=pltpu.VMEM)] * 2,
        out_specs=pl.BlockSpec(memory_space=pltpu.VMEM),
        scratch_shapes=[
            pltpu.VMEM((n, groups * slots, 128), F32),
            pltpu.VMEM((n, groups * slots, 128), F32),
            pltpu.VMEM((4 * slots, 128), F32),
            pltpu.VMEM((chunks, 2, 2, layers, width, columns), F32),
            pltpu.VMEM((chunks, 2, layers, width, columns), F32),
            pltpu.VMEM((chunks, layers, width, columns), F32),
            pltpu.VMEM((layers, chunks, width, columns), F32),
            dma((n,)), dma((n,)),
            dma((chunks,)), dma((chunks,)),
            dma((chunks,)), dma((chunks,)),
            dma((layers, chunks)), dma((layers, chunks)),
        ],
        compiler_params=pltpu.CompilerParams(
            collective_id=0, has_side_effects=True, vmem_limit_bytes=58 * 1024 * 1024
        ),
        name="exchanged_sums",
    )(dense, legs)


def row_kernel(
    count_ref, spectra_ref, fcos_ref, fsin_ref, ccos_ref, csin_ref, wide_ref, absorb_ref, resp_ref, out_ref,
    high_ref, low_ref, rhigh_ref, rlow_ref,
):
    step = pl.program_id(0)
    waves = fcos_ref.shape[1]
    levels = absorb_ref.shape[1]
    points = fcos_ref.shape[0]

    @pl.when(step == 0)
    def _():
        even = spectra_ref[pl.ds(0, waves, stride=2), :]
        odd = spectra_ref[pl.ds(1, waves, stride=2), :]
        half = even.shape[1] // 2
        real = jnp.concatenate((even[:, :half], odd[:, :half]), axis=1)
        imag = jnp.concatenate((even[:, half:], odd[:, half:]), axis=1)
        wide = wide_ref[...]
        for index, piece in enumerate((real, imag)):
            high, low = split(dot3(piece, wide))
            high_ref[pl.ds(index * waves, waves), :] = high
            low_ref[pl.ds(index * waves, waves), :] = low
        high, low = split(resp_ref[...])
        rhigh_ref[pl.ds(0, levels), :] = high
        rhigh_ref[pl.ds(levels, levels), :] = high
        rlow_ref[...] = low

    base_c = ccos_ref[pl.ds(step, 1), :]
    base_s = csin_ref[pl.ds(step, 1), :]
    fine_c = fcos_ref[...]
    fine_s = fsin_ref[...]
    cosine = base_c * fine_c - base_s * fine_s
    sine = -(base_s * fine_c + base_c * fine_s)
    lookup_high, lookup_low = split(jnp.concatenate((cosine, sine), axis=1))
    high = high_ref[...]
    temps = dot(lookup_high, high) + dot(lookup_low, high) + dot(lookup_high, low_ref[...])
    temps = jnp.concatenate((temps[:, :levels], temps[:, levels:]), axis=0)

    source = jnp.exp(0.5 * temps)
    layers = absorb_ref[...] * source
    before = lax.broadcasted_iota(jnp.int32, (2 * levels, levels), 0) % levels
    after = lax.broadcasted_iota(jnp.int32, (2 * levels, levels), 1)
    upper = jnp.where(before < after, 1.0, 0.0).astype(BF16)
    layers_high, layers_low = split(layers)
    above = dot(jnp.concatenate((layers_high, layers_low), axis=1), upper)
    emitted = source * jnp.exp(-above) * (1.0 - jnp.exp(-layers))
    place = step * points + lax.broadcasted_iota(jnp.int32, (2 * points, levels), 0) % points
    emitted = jnp.where(place < count_ref[0], emitted, 0.0)
    emitted_high, emitted_low = split(emitted)
    bright = dot(jnp.concatenate((emitted_high, emitted_low), axis=1), rhigh_ref[...])
    bright = bright + dot(emitted_high, rlow_ref[...])
    out_ref[0, 0] = bright[:points]
    out_ref[0, 1] = bright[points:]


def row_tables(row_count, waves, points):
    orders = jnp.arange(waves, dtype=jnp.int32)

    def angles(places):
        phases = places[:, None] * orders[None, :] % row_count
        return 2.0 * math.pi * phases.astype(F32) / row_count.astype(F32)

    fine = angles(jnp.arange(FINE, dtype=jnp.int32))
    coarse = angles(FINE * jnp.arange(points // FINE, dtype=jnp.int32))
    weights = jnp.where(orders == 0, 1.0, 2.0) * (2 * orders < row_count).astype(F32)
    return jnp.cos(fine), jnp.sin(fine), weights * jnp.cos(coarse), weights * jnp.sin(coarse)


def synthesize_row(spectra, row_counts, basis, absorb, kernel, points):
    waves = spectra.shape[0] // 2
    levels, channels = kernel.shape
    columns = spectra.shape[1]
    fcos, fsin, ccos, csin = row_tables(row_counts[0], waves, points)
    top = jnp.concatenate((basis, basis), axis=1)
    wide = jnp.concatenate((top, jnp.concatenate((basis, -basis), axis=1)), axis=0)
    steps = points // FINE

    def whole(*shape):
        return pl.BlockSpec(shape, lambda i, *_: (0,) * len(shape))

    return pl.pallas_call(
        row_kernel,
        out_shape=jax.ShapeDtypeStruct((1, 2, points, channels), F32),
        grid_spec=pltpu.PrefetchScalarGridSpec(
            num_scalar_prefetch=1,
            grid=(steps,),
            in_specs=[
                whole(2 * waves, columns),
                whole(FINE, waves),
                whole(FINE, waves),
                whole(steps, waves),
                whole(steps, waves),
                whole(*wide.shape),
                whole(1, levels),
                whole(levels, channels),
            ],
            out_specs=pl.BlockSpec((1, 2, FINE, channels), lambda i, *_: (0, 0, i, 0)),
            scratch_shapes=[
                pltpu.VMEM((2 * waves, 2 * levels), BF16),
                pltpu.VMEM((2 * waves, 2 * levels), BF16),
                pltpu.VMEM((2 * levels, channels), BF16),
                pltpu.VMEM((levels, channels), BF16),
            ],
        ),
        name="row_synthesis",
    )(row_counts, spectra, fcos, fsin, ccos, csin, wide, absorb[None, :], kernel)


def moved_coefficients(coefficients, legendre):
    waves, _, slots, _ = coefficients.shape
    first = lax.axis_index("spec") * slots
    spread = prior_spread(jnp.arange(waves, dtype=jnp.int32), first + jnp.arange(slots, dtype=jnp.int32), waves)
    scaled = coefficients.astype(F32) * spread[..., None]
    spectral = lax.all_to_all(scaled, "spec", split_axis=0, concat_axis=2, tiled=True)
    sums = jnp.einsum("mpsj,mpsc->mpjc", legendre, spectral, precision=PRECISE)
    sums = lax.all_to_all(sums, "spec", split_axis=2, concat_axis=0, tiled=True)
    return sums.reshape(2 * waves, sums.shape[-1])


def on_device(coefficients, legendre, row_counts, basis, absorb, peak_level, width):
    kernel = channel_kernel(peak_level, width, basis.shape[1])
    own, _, every, rows = legendre.shape
    waves, _, slots, columns = coefficients.shape
    n = waves // own
    fits = n == rows and n % 8 == 0 and 128 % n == 0 and every == n * slots and columns == 128
    fits = fits and (128 // n) % 8 == 0 and own % (128 // n) == 0 and slots % 4 == 0
    if fits and (slots * 128 // n) % 16 == 0 and 2 * waves >= 2 * slots * n:
        spectra = exchanged_sums(coefficients, legendre, n)
    else:
        spectra = moved_coefficients(coefficients, legendre)
    return synthesize_row(spectra, row_counts, basis, absorb, kernel, NLON)


def solution(mesh):
    placed = (
        P("draws", None, "spec", None),
        P("spec", None, None, None),
        P("spec"),
        P(),
        P(),
        P(),
        P(),
    )
    return jax.shard_map(
        on_device,
        mesh=mesh,
        in_specs=placed,
        out_specs=P(("draws", "spec"), None, None, None),
        check_vma=False,
    )
```

```python
import functools
import math

import jax
import jax.numpy as jnp
from jax import lax
from jax.experimental import pallas as pl
from jax.experimental.pallas import tpu as pltpu
from jax.sharding import PartitionSpec as P

NLON = 1280
FINE = 128

PRECISE = lax.Precision.HIGHEST
F32 = jnp.float32
BF16 = jnp.bfloat16


def prior_spread(orders, slots, waves):
    parity = jnp.arange(2, dtype=jnp.int32)[None, :, None]
    degree = orders[:, None, None] + 2 * slots[None, None, :] + parity
    spread = lax.rsqrt((degree + 1).astype(F32) * waves)
    return jnp.where(degree < waves, spread, jnp.zeros_like(spread))


def split(x):
    high = x.astype(BF16)
    return high, (x - high.astype(F32)).astype(BF16)


def dot(a, b):
    return jnp.dot(a, b, preferred_element_type=F32)


def dot3(a, b):
    ah, al = split(a)
    bh, bl = split(b)
    return dot(ah, bh) + dot(al, bh) + dot(ah, bl)


def place_in_ring(n):
    me = lax.axis_index("spec")
    core = me % 2
    side = (me // 2) % 2
    layer = me // 4
    return me, core, side, layer


def exchange_kernel(
    n, draws, waves, coef_hbm, leg_ref, out_ref, coef_ref, send_ref, legs_ref, wide_ref, sums_ref, near_ref, side_ref,
    far_ref, coef_sem, leg_send, leg_recv, pass_send, near_send, near_recv, side_send, side_recv, far_send, far_recv,
):
    me, core, side, layer = place_in_ring(n)
    layers = n // 4
    chunks = n
    chip = me // 2
    draw = lax.axis_index("draws")
    rows = n
    columns = coef_hbm.shape[1]
    every = leg_ref.shape[1]
    slots = every // n
    lanes = 128
    pairs = lanes // rows
    per = pairs // 2
    own = waves // n
    groups = own // per
    depth = per * slots * 2
    part = groups * pairs
    partner = me + 1 - 2 * core
    across = me + 2 - 4 * side

    def spot(z, y, c):
        return (z * 2 + y) * 2 + c

    def remote(src, dst, send_sem, recv_sem, target):
        return pltpu.make_async_remote_copy(
            src_ref=src, dst_ref=dst, send_sem=send_sem, recv_sem=recv_sem,
            device_id={"spec": target}, device_id_type=pl.DeviceIdType.MESH,
        )

    def leg_copy(source, target):
        return remote(send_ref.at[target], legs_ref.at[source], leg_send.at[target], leg_recv.at[source], target)

    def pass_copy(source):
        return pltpu.make_async_remote_copy(
            src_ref=legs_ref.at[source], dst_ref=legs_ref.at[source],
            send_sem=pass_send.at[source], recv_sem=leg_recv.at[source],
            device_id={"draws": 1 - draw}, device_id_type=pl.DeviceIdType.MESH,
        )

    def near_copy(q):
        return remote(sums_ref.at[q, 1 - core], near_ref.at[q], near_send.at[q], near_recv.at[q], partner)

    def side_copy(q):
        return remote(sums_ref.at[q, core, 1 - side], side_ref.at[q], side_send.at[q], side_recv.at[q], across)

    def far_copy(q, source, target):
        return remote(
            sums_ref.at[q, core, side, target], far_ref.at[source, q],
            far_send.at[target, q], far_recv.at[source, q], spot(target, side, core),
        )

    others = [(dz, dy, dc) for dz in range(layers) for dy in range(2) for dc in range(2)][1:]

    def other(offset):
        dz, dy, dc = offset
        return spot((layer + dz) % layers, (side + dy) % 2, (core + dc) % 2)

    coef_copy = pltpu.make_async_copy(coef_hbm, coef_ref, coef_sem)
    coef_copy.start()
    paired = draws == 2
    barrier = pltpu.get_barrier_semaphore()
    if paired:
        pl.semaphore_signal(barrier, inc=1, device_id={"draws": 1 - draw}, device_id_type=pl.DeviceIdType.MESH)
    for offset in others:
        pl.semaphore_signal(barrier, inc=1, device_id={"spec": other(offset)}, device_id_type=pl.DeviceIdType.MESH)

    row = lax.broadcasted_iota(jnp.int32, (lanes, lanes), 0)
    lane = lax.broadcasted_iota(jnp.int32, (lanes, lanes), 1)
    row_at = row % rows
    ordered = ((row_at % 2) * 2 + (row_at // 2) % 2) * layers + row_at // 4
    moves = jnp.where(ordered * pairs + row // rows == lane, 1.0, 0.0)
    leg_row = lax.broadcasted_iota(jnp.int32, (lanes, every), 0) // rows
    leg_slot = lax.broadcasted_iota(jnp.int32, (lanes, every), 1)
    degree_part = leg_row // 2 + leg_row % 2 + 2 * leg_slot

    @pl.loop(0, groups // 2)
    def _(double):
        turned = []
        for half in range(2):
            g = double * 2 + half
            degree = degree_part + (me * own + g * per)
            spread = lax.rsqrt((degree + 1).astype(F32) * float(waves))
            spread = jnp.where(degree < waves, spread, 0.0)
            values = leg_ref[pl.ds(pl.multiple_of(g * lanes, lanes), lanes), :] * spread
            turned.append(
                lax.dot_general(
                    values, moves, (((0,), (0,)), ((), ())), precision=PRECISE, preferred_element_type=F32
                )
            )
        for k in range(n):
            piece = [t[k * slots:(k + 1) * slots] for t in turned]
            send_ref[k, pl.ds(pl.multiple_of(double * 2 * slots, 2 * slots), 2 * slots), :] = jnp.concatenate(piece, 0)

    pl.semaphore_wait(barrier, len(others) + paired)
    sends = (core == draw) if paired else (core >= 0)
    for offset in others:
        target = other(offset)

        @pl.when(jnp.logical_and(sends, me + target < n))
        def _():
            leg_copy(me, target).start()

    legs_ref[me] = send_ref[me]
    coef_copy.wait()

    def receive(owner):
        wanted = jnp.logical_and(owner != me, me + owner < n)
        if not paired:
            return

        @pl.when(jnp.logical_and(wanted, owner % 2 == draw))
        def _():
            leg_copy(owner, me).wait_recv()
            pass_copy(owner).start()

    expand_row = lax.broadcasted_iota(jnp.int32, (depth, lanes), 0)
    expand_lane = lax.broadcasted_iota(jnp.int32, (depth, lanes), 1) % pairs
    keep = (expand_row // (2 * slots)) * 2 + expand_row % 2 == expand_lane

    def partial(q):
        owner = q

        @pl.when(me + owner < n)
        def _():
            waits = owner != me
            if paired:
                waits = jnp.logical_and(waits, owner % 2 != draw)

            @pl.when(waits)
            def _():
                leg_copy(owner, me).wait_recv()

            @pl.loop(0, groups // 2)
            def _(double):
                legs = legs_ref[owner, pl.ds(pl.multiple_of(double * 2 * slots, 2 * slots), 2 * slots), :]
                wide_ref[pl.ds(0, 2 * slots, stride=2), :] = legs
                wide_ref[pl.ds(1, 2 * slots, stride=2), :] = legs
                for half in range(2):
                    g = owner * groups + double * 2 + half
                    values = coef_ref[pl.ds(pl.multiple_of(g * depth, depth), depth), :]
                    one = wide_ref[pl.ds(half * 2 * slots, 2 * slots), :]
                    tiled = jnp.where(keep, jnp.concatenate([one] * per, axis=0), 0.0)
                    both = jnp.concatenate(split(tiled), axis=1)
                    sums = lax.dot_general(both, values, (((0,), (0,)), ((), ())), preferred_element_type=F32)
                    sums = (sums[:lanes] + sums[lanes:]).reshape(2, 2, layers, pairs, columns)
                    at = pl.multiple_of((double * 2 + half) * pairs, pairs)
                    sums_ref[q, :, :, :, pl.ds(at, pairs), :] = sums

        @pl.when(me + owner >= n)
        def _():
            sums_ref[q] = jnp.zeros((2, 2, layers, part, columns), F32)

    def compute(q):
        @pl.when(q + 2 * chip < chunks)
        def _():
            partial(q)
            near_copy(q).start()

    def merge_near(q):
        @pl.when(q + 2 * chip < chunks)
        def _():
            near_copy(q).wait_recv()

            for y in (0, 1):
                @pl.loop(0, layers)
                def _(z):
                    sums_ref[q, core, y, z] += near_ref[q, y, z]

            side_copy(q).start()

    def merge_side(q):
        here = q + 2 * chip < chunks
        there = q + 2 * (across // 2) < chunks

        @pl.when(there)
        def _():
            side_copy(q).wait_recv()

        @pl.when(jnp.logical_and(here, there))
        def _():
            @pl.loop(0, layers)
            def _(z):
                sums_ref[q, core, side, z] += side_ref[q, z]

        @pl.when(jnp.logical_and(jnp.logical_not(here), there))
        def _():
            @pl.loop(0, layers)
            def _(z):
                sums_ref[q, core, side, z] = side_ref[q, z]

        @pl.when(jnp.logical_or(here, there))
        def _():
            for dz in range(1, layers):
                far_copy(q, layer, (layer + dz) % layers).start()

    lag = min(7, chunks)
    ahead = 2
    for owner in range(ahead):
        receive(owner)

    @pl.loop(0, chunks + 1)
    def _(t):
        @pl.when(t + ahead < chunks)
        def _():
            receive(t + ahead)

        @pl.when(t < chunks)
        def _():
            compute(t)

        @pl.when(t >= 1)
        def _():
            merge_near(t - 1)

        @pl.when(t >= lag)
        def _():
            merge_side(t - lag)

    @pl.loop(chunks + 1 - lag, chunks)
    def _(q):
        merge_side(q)

    @pl.loop(0, chunks)
    def _(q):
        at = pl.ds(pl.multiple_of(q * part, part), part)

        @pl.when(q + 4 * layer < chunks)
        def _():
            out_ref[at, :] = sums_ref[q, core, side, layer]

        @pl.when(q + 4 * layer >= chunks)
        def _():
            out_ref[at, :] = jnp.zeros((part, columns), F32)

        for dz in range(1, layers):
            source = (layer + dz) % layers

            @pl.when(q + 4 * source < chunks)
            def _():
                far_copy(q, source, layer).wait_recv()
                out_ref[at, :] += far_ref[source, q]

    for offset in others:
        target = other(offset)

        @pl.when(jnp.logical_and(sends, me + target < n))
        def _():
            leg_copy(me, target).wait_send()

    if paired:
        @pl.loop(0, n)
        def _(owner):
            @pl.when(jnp.logical_and(owner != me, jnp.logical_and(me + owner < n, owner % 2 == draw)))
            def _():
                pass_copy(owner).wait_send()

    @pl.loop(0, chunks)
    def _(q):
        @pl.when(q + 2 * chip < chunks)
        def _():
            near_copy(q).wait_send()
            side_copy(q).wait_send()

        @pl.when(q + 4 * layer < chunks)
        def _():
            for dz in range(1, layers):
                far_copy(q, layer, (layer + dz) % layers).wait_send()


def exchanged_sums(coefficients, legendre, n, draws):
    waves, _, slots, columns = coefficients.shape
    own, _, every, rows = legendre.shape
    dense = jnp.transpose(coefficients, (0, 2, 1, 3)).reshape(waves * slots * 2, columns)
    legs = jnp.transpose(legendre, (0, 1, 3, 2)).reshape(own * 2 * rows, every)
    layers, chunks = n // 4, n
    pairs = 128 // rows
    groups = own * 2 // pairs
    width = groups * pairs
    dma = pltpu.SemaphoreType.DMA

    def body(*refs):
        exchange_kernel(n, draws, waves, *refs)

    return pl.pallas_call(
        body,
        out_shape=jax.ShapeDtypeStruct((2 * waves, columns), F32),
        in_specs=[pl.BlockSpec(memory_space=pl.ANY), pl.BlockSpec(memory_space=pltpu.VMEM)],
        out_specs=pl.BlockSpec(memory_space=pltpu.VMEM),
        scratch_shapes=[
            pltpu.VMEM(dense.shape, BF16),
            pltpu.VMEM((n, groups * slots, 128), F32),
            pltpu.VMEM((n, groups * slots, 128), F32),
            pltpu.VMEM((4 * slots, 128), F32),
            pltpu.VMEM((chunks, 2, 2, layers, width, columns), F32),
            pltpu.VMEM((chunks, 2, layers, width, columns), F32),
            pltpu.VMEM((chunks, layers, width, columns), F32),
            pltpu.VMEM((layers, chunks, width, columns), F32),
            dma, dma((n,)), dma((n,)), dma((n,)),
            dma((chunks,)), dma((chunks,)),
            dma((chunks,)), dma((chunks,)),
            dma((layers, chunks)), dma((layers, chunks)),
        ],
        compiler_params=pltpu.CompilerParams(
            collective_id=0, has_side_effects=True, vmem_limit_bytes=58 * 1024 * 1024
        ),
        name="exchanged_sums",
    )(dense, legs)


def row_kernel(
    count_ref, spectra_ref, basis_ref, absorb_ref, peak_ref, width_ref, out_ref,
    fcos_ref, fsin_ref, ccos_ref, csin_ref, high_ref, low_ref, rhigh_ref, rlow_ref,
):
    step = pl.program_id(0)
    waves = fcos_ref.shape[1]
    levels = absorb_ref.shape[1]
    points = fcos_ref.shape[0]
    tiny = 16
    middle = points // tiny

    @pl.when(step == 0)
    def _():
        count = count_ref[0].astype(F32)
        table = (tiny + middle + ccos_ref.shape[0], waves)
        index = lax.broadcasted_iota(jnp.int32, table, 0)
        order = lax.broadcasted_iota(jnp.int32, table, 1)
        places = jnp.where(index < tiny, index, (index - tiny) * tiny)
        places = jnp.where(index < tiny + middle, places, (index - tiny - middle) * points)
        phases = (places * order).astype(F32)
        phases = phases - jnp.floor(phases / count) * count
        angles = 2.0 * math.pi * phases / count
        cosine, sine = jnp.cos(angles), jnp.sin(angles)
        weights = jnp.where(order == 0, 1.0, 2.0) * jnp.where(2 * order < count_ref[0], 1.0, 0.0)
        first = tiny + middle
        ccos_ref[...] = (cosine * weights)[first:]
        csin_ref[...] = (sine * weights)[first:]
        for b in range(middle):
            turn_c, turn_s = cosine[tiny + b:tiny + b + 1], sine[tiny + b:tiny + b + 1]
            fcos_ref[pl.ds(b * tiny, tiny), :] = cosine[:tiny] * turn_c - sine[:tiny] * turn_s
            fsin_ref[pl.ds(b * tiny, tiny), :] = sine[:tiny] * turn_c + cosine[:tiny] * turn_s

        even = spectra_ref[pl.ds(0, waves, stride=2), :]
        odd = spectra_ref[pl.ds(1, waves, stride=2), :]
        half = even.shape[1] // 2
        real = jnp.concatenate((even[:, :half], odd[:, :half]), axis=1)
        imag = jnp.concatenate((even[:, half:], odd[:, half:]), axis=1)
        basis = basis_ref[...]
        top = jnp.concatenate((basis, basis), axis=1)
        wide = jnp.concatenate((top, jnp.concatenate((basis, -basis), axis=1)), axis=0)
        for index, piece in enumerate((real, imag)):
            high, low = split(dot3(piece, wide))
            high_ref[pl.ds(index * waves, waves), :] = high
            low_ref[pl.ds(index * waves, waves), :] = low
        height = lax.broadcasted_iota(jnp.int32, rlow_ref.shape, 0)
        offsets = (height - peak_ref[...]).astype(F32) / width_ref[...]
        shape = jnp.exp(-offsets * offsets)
        high, low = split(shape / jnp.sum(shape, axis=0, keepdims=True))
        rhigh_ref[pl.ds(0, levels), :] = high
        rhigh_ref[pl.ds(levels, levels), :] = high
        rlow_ref[...] = low

    base_c = ccos_ref[pl.ds(step, 1), :]
    base_s = csin_ref[pl.ds(step, 1), :]
    fine_c = fcos_ref[...]
    fine_s = fsin_ref[...]
    cosine = base_c * fine_c - base_s * fine_s
    sine = -(base_s * fine_c + base_c * fine_s)
    lookup_high, lookup_low = split(jnp.concatenate((cosine, sine), axis=1))
    high = high_ref[...]
    temps = dot(lookup_high, high) + dot(lookup_low, high) + dot(lookup_high, low_ref[...])
    temps = jnp.concatenate((temps[:, :levels], temps[:, levels:]), axis=0)

    source = jnp.exp(0.5 * temps)
    layers = absorb_ref[...] * source
    before = lax.broadcasted_iota(jnp.int32, (2 * levels, levels), 0) % levels
    after = lax.broadcasted_iota(jnp.int32, (2 * levels, levels), 1)
    upper = jnp.where(before < after, 1.0, 0.0).astype(BF16)
    layers_high, layers_low = split(layers)
    above = dot(jnp.concatenate((layers_high, layers_low), axis=1), upper)
    emitted = source * jnp.exp(-above) * (1.0 - jnp.exp(-layers))
    place = step * points + lax.broadcasted_iota(jnp.int32, (2 * points, levels), 0) % points
    emitted = jnp.where(place < count_ref[0], emitted, 0.0)
    emitted_high, emitted_low = split(emitted)
    bright = dot(jnp.concatenate((emitted_high, emitted_low), axis=1), rhigh_ref[...])
    bright = bright + dot(emitted_high, rlow_ref[...])
    out_ref[0, 0] = bright[:points]
    out_ref[0, 1] = bright[points:]


def synthesize_row(spectra, row_counts, basis, absorb, peak_level, width, points):
    waves = spectra.shape[0] // 2
    levels, channels = absorb.shape[0], width.shape[0]
    columns = spectra.shape[1]
    steps = points // FINE
    coarse = -(-steps // 8) * 8

    def whole(*shape):
        return pl.BlockSpec(shape, lambda i, *_: (0,) * len(shape))

    return pl.pallas_call(
        row_kernel,
        out_shape=jax.ShapeDtypeStruct((1, 2, points, channels), F32),
        grid_spec=pltpu.PrefetchScalarGridSpec(
            num_scalar_prefetch=1,
            grid=(steps,),
            in_specs=[
                whole(2 * waves, columns),
                whole(*basis.shape),
                whole(1, levels),
                whole(1, channels),
                whole(1, channels),
            ],
            out_specs=pl.BlockSpec((1, 2, FINE, channels), lambda i, *_: (0, 0, i, 0)),
            scratch_shapes=[
                pltpu.VMEM((FINE, waves), F32),
                pltpu.VMEM((FINE, waves), F32),
                pltpu.VMEM((coarse, waves), F32),
                pltpu.VMEM((coarse, waves), F32),
                pltpu.VMEM((2 * waves, 2 * levels), BF16),
                pltpu.VMEM((2 * waves, 2 * levels), BF16),
                pltpu.VMEM((2 * levels, channels), BF16),
                pltpu.VMEM((levels, channels), BF16),
            ],
        ),
        name="row_synthesis",
    )(row_counts, spectra, basis, absorb[None, :], peak_level[None, :], width[None, :])


def moved_coefficients(coefficients, legendre):
    waves, _, slots, _ = coefficients.shape
    first = lax.axis_index("spec") * slots
    spread = prior_spread(jnp.arange(waves, dtype=jnp.int32), first + jnp.arange(slots, dtype=jnp.int32), waves)
    scaled = coefficients.astype(F32) * spread[..., None]
    spectral = lax.all_to_all(scaled, "spec", split_axis=0, concat_axis=2, tiled=True)
    sums = jnp.einsum("mpsj,mpsc->mpjc", legendre, spectral, precision=PRECISE)
    sums = lax.all_to_all(sums, "spec", split_axis=2, concat_axis=0, tiled=True)
    return sums.reshape(2 * waves, sums.shape[-1])


def on_device(draws, coefficients, legendre, row_counts, basis, absorb, peak_level, width):
    own, _, every, rows = legendre.shape
    waves, _, slots, columns = coefficients.shape
    n = waves // own
    fits = n == rows and n % 8 == 0 and 128 % n == 0 and every == n * slots and columns == 128
    fits = fits and (128 // n) % 8 == 0 and own % (128 // n) == 0 and slots % 4 == 0
    if fits and (slots * 128 // n) % 16 == 0 and 2 * waves >= 2 * slots * n:
        spectra = exchanged_sums(coefficients, legendre, n, draws)
    else:
        spectra = moved_coefficients(coefficients, legendre)
    return synthesize_row(spectra, row_counts, basis, absorb, peak_level, width, NLON)


def solution(mesh):
    placed = (
        P("draws", None, "spec", None),
        P("spec", None, None, None),
        P("spec"),
        P(),
        P(),
        P(),
        P(),
    )
    return jax.shard_map(
        functools.partial(on_device, mesh.shape["draws"]),
        mesh=mesh,
        in_specs=placed,
        out_specs=P(("draws", "spec"), None, None, None),
        check_vma=False,
    )
```

```python
import functools
import math

import jax
import jax.numpy as jnp
from jax import lax
from jax.experimental import pallas as pl
from jax.experimental.pallas import tpu as pltpu
from jax.sharding import PartitionSpec as P

NLON = 1280
FINE = 256
BLOCK = 128

PRECISE = lax.Precision.HIGHEST
F32 = jnp.float32
BF16 = jnp.bfloat16


def prior_spread(orders, slots, waves):
    parity = jnp.arange(2, dtype=jnp.int32)[None, :, None]
    degree = orders[:, None, None] + 2 * slots[None, None, :] + parity
    spread = lax.rsqrt((degree + 1).astype(F32) * waves)
    return jnp.where(degree < waves, spread, jnp.zeros_like(spread))


def split(x):
    high = x.astype(BF16)
    return high, (x - high.astype(F32)).astype(BF16)


def dot(a, b):
    return jnp.dot(a, b, preferred_element_type=F32)


def dot3(a, b):
    ah, al = split(a)
    bh, bl = split(b)
    return dot(ah, bh) + dot(al, bh) + dot(ah, bl)


def place_in_ring(n):
    me = lax.axis_index("spec")
    core = me % 2
    side = (me // 2) % 2
    layer = me // 4
    return me, core, side, layer


def exchange_kernel(
    n, draws, waves, count_ref, coef_hbm, leg_ref, basis_ref, out_ref, coef_ref, send_ref, legs_ref, wide_ref, sums_ref, near_ref, side_ref,
    far_ref, held_ref, fcos_ref, fsin_ref, coef_sem, leg_send, leg_recv, pass_send, near_send, near_recv, side_send, side_recv, far_send, far_recv,
):
    me, core, side, layer = place_in_ring(n)
    layers = n // 4
    chunks = n
    chip = me // 2
    draw = lax.axis_index("draws")
    rows = n
    columns = coef_hbm.shape[1]
    every = leg_ref.shape[1]
    slots = every // n
    lanes = 128
    pairs = lanes // rows
    per = pairs // 2
    own = waves // n
    groups = own // per
    depth = per * slots * 2
    part = groups * pairs
    partner = me + 1 - 2 * core
    across = me + 2 - 4 * side

    def spot(z, y, c):
        return (z * 2 + y) * 2 + c

    def remote(src, dst, send_sem, recv_sem, target):
        return pltpu.make_async_remote_copy(
            src_ref=src, dst_ref=dst, send_sem=send_sem, recv_sem=recv_sem,
            device_id={"spec": target}, device_id_type=pl.DeviceIdType.MESH,
        )

    def leg_copy(source, target):
        return remote(send_ref.at[target], legs_ref.at[source], leg_send.at[target], leg_recv.at[source], target)

    def pass_copy(source):
        return pltpu.make_async_remote_copy(
            src_ref=legs_ref.at[source], dst_ref=legs_ref.at[source],
            send_sem=pass_send.at[source], recv_sem=leg_recv.at[source],
            device_id={"draws": 1 - draw}, device_id_type=pl.DeviceIdType.MESH,
        )

    def near_copy(q):
        return remote(sums_ref.at[q, 1 - core], near_ref.at[q], near_send.at[q], near_recv.at[q], partner)

    def side_copy(q):
        return remote(sums_ref.at[q, core, 1 - side], side_ref.at[q], side_send.at[q], side_recv.at[q], across)

    def far_copy(q, source, target):
        return remote(
            sums_ref.at[q, core, side, target], far_ref.at[source, q],
            far_send.at[target, q], far_recv.at[source, q], spot(target, side, core),
        )

    others = [(dz, dy, dc) for dz in range(layers) for dy in range(2) for dc in range(2)][1:]

    def other(offset):
        dz, dy, dc = offset
        return spot((layer + dz) % layers, (side + dy) % 2, (core + dc) % 2)

    coef_copy = pltpu.make_async_copy(coef_hbm, coef_ref, coef_sem)
    coef_copy.start()
    paired = draws == 2
    barrier = pltpu.get_barrier_semaphore()
    if paired:
        pl.semaphore_signal(barrier, inc=1, device_id={"draws": 1 - draw}, device_id_type=pl.DeviceIdType.MESH)
    for offset in others:
        pl.semaphore_signal(barrier, inc=1, device_id={"spec": other(offset)}, device_id_type=pl.DeviceIdType.MESH)

    row = lax.broadcasted_iota(jnp.int32, (lanes, lanes), 0)
    lane = lax.broadcasted_iota(jnp.int32, (lanes, lanes), 1)
    row_at = row % rows
    ordered = ((row_at % 2) * 2 + (row_at // 2) % 2) * layers + row_at // 4
    moves = jnp.where(ordered * pairs + row // rows == lane, 1.0, 0.0)
    leg_row = lax.broadcasted_iota(jnp.int32, (lanes, every), 0) // rows
    leg_slot = lax.broadcasted_iota(jnp.int32, (lanes, every), 1)
    degree_part = leg_row // 2 + leg_row % 2 + 2 * leg_slot

    @pl.loop(0, groups // 2)
    def _(double):
        turned = []
        for half in range(2):
            g = double * 2 + half
            degree = degree_part + (me * own + g * per)
            spread = lax.rsqrt((degree + 1).astype(F32) * float(waves))
            spread = jnp.where(degree < waves, spread, 0.0)
            values = leg_ref[pl.ds(pl.multiple_of(g * lanes, lanes), lanes), :] * spread
            turned.append(
                lax.dot_general(
                    values, moves, (((0,), (0,)), ((), ())), precision=PRECISE, preferred_element_type=F32
                )
            )
        for k in range(n):
            piece = [t[k * slots:(k + 1) * slots] for t in turned]
            send_ref[k, pl.ds(pl.multiple_of(double * 2 * slots, 2 * slots), 2 * slots), :] = jnp.concatenate(piece, 0)

    pl.semaphore_wait(barrier, len(others) + paired)
    sends = (core == draw) if paired else (core >= 0)
    for offset in others:
        target = other(offset)

        @pl.when(jnp.logical_and(sends, me + target < n))
        def _():
            leg_copy(me, target).start()

    legs_ref[me] = send_ref[me]
    coef_copy.wait()

    def receive(owner):
        wanted = jnp.logical_and(owner != me, me + owner < n)
        if not paired:
            return

        @pl.when(jnp.logical_and(wanted, owner % 2 == draw))
        def _():
            leg_copy(owner, me).wait_recv()
            pass_copy(owner).start()

    expand_row = lax.broadcasted_iota(jnp.int32, (depth, lanes), 0)
    expand_lane = lax.broadcasted_iota(jnp.int32, (depth, lanes), 1) % pairs
    keep = (expand_row // (2 * slots)) * 2 + expand_row % 2 == expand_lane

    def partial(q):
        owner = q

        @pl.when(me + owner < n)
        def _():
            waits = owner != me
            if paired:
                waits = jnp.logical_and(waits, owner % 2 != draw)

            @pl.when(waits)
            def _():
                leg_copy(owner, me).wait_recv()

            @pl.loop(0, groups // 2)
            def _(double):
                legs = legs_ref[owner, pl.ds(pl.multiple_of(double * 2 * slots, 2 * slots), 2 * slots), :]
                wide_ref[pl.ds(0, 2 * slots, stride=2), :] = legs
                wide_ref[pl.ds(1, 2 * slots, stride=2), :] = legs
                for half in range(2):
                    g = owner * groups + double * 2 + half
                    values = coef_ref[pl.ds(pl.multiple_of(g * depth, depth), depth), :]
                    one = wide_ref[pl.ds(half * 2 * slots, 2 * slots), :]
                    tiled = jnp.where(keep, jnp.concatenate([one] * per, axis=0), 0.0)
                    both = jnp.concatenate(split(tiled), axis=1)
                    sums = lax.dot_general(both, values, (((0,), (0,)), ((), ())), preferred_element_type=F32)
                    sums = (sums[:lanes] + sums[lanes:]).reshape(2, 2, layers, pairs, columns)
                    at = pl.multiple_of((double * 2 + half) * pairs, pairs)
                    sums_ref[q, :, :, :, pl.ds(at, pairs), :] = sums

        @pl.when(me + owner >= n)
        def _():
            sums_ref[q] = jnp.zeros((2, 2, layers, part, columns), F32)

    def compute(q):
        @pl.when(q + 2 * chip < chunks)
        def _():
            partial(q)
            near_copy(q).start()

    def merge_near(q):
        @pl.when(q + 2 * chip < chunks)
        def _():
            near_copy(q).wait_recv()

            for y in (0, 1):
                @pl.loop(0, layers)
                def _(z):
                    sums_ref[q, core, y, z] += near_ref[q, y, z]

            side_copy(q).start()

    def merge_side(q):
        here = q + 2 * chip < chunks
        there = q + 2 * (across // 2) < chunks

        @pl.when(there)
        def _():
            side_copy(q).wait_recv()

        @pl.when(jnp.logical_and(here, there))
        def _():
            @pl.loop(0, layers)
            def _(z):
                sums_ref[q, core, side, z] += side_ref[q, z]

        @pl.when(jnp.logical_and(jnp.logical_not(here), there))
        def _():
            @pl.loop(0, layers)
            def _(z):
                sums_ref[q, core, side, z] = side_ref[q, z]

        @pl.when(jnp.logical_or(here, there))
        def _():
            for dz in range(1, layers):
                far_copy(q, layer, (layer + dz) % layers).start()

    points = out_ref.shape[0]
    tiny = 16
    middle = BLOCK // tiny
    both_waves = 2 * own
    table = (tiny + middle + -(-points // BLOCK // 8) * 8, 2 * both_waves)
    first = tiny + middle
    out_ref[...] = jnp.zeros_like(out_ref)

    def collect(q, which):
        at = pl.ds(which * part, part)

        @pl.when(q + 4 * layer < chunks)
        def _():
            held_ref[at, :] = sums_ref[q, core, side, layer]

        @pl.when(q + 4 * layer >= chunks)
        def _():
            held_ref[at, :] = jnp.zeros((part, columns), F32)

        for dz in range(1, layers):
            source = (layer + dz) % layers

            @pl.when(q + 4 * source < chunks)
            def _():
                far_copy(q, source, layer).wait_recv()
                held_ref[at, :] += far_ref[source, q]

    def finish(pair):
        count = count_ref[0]
        index = lax.broadcasted_iota(jnp.int32, table, 0)
        lane_at = lax.broadcasted_iota(jnp.int32, table, 1)
        imaginary = lane_at >= both_waves
        order = pair * both_waves + jnp.where(imaginary, lane_at - both_waves, lane_at)
        places = jnp.where(index < tiny, index, (index - tiny) * tiny)
        places = jnp.where(index < first, places, (index - first) * BLOCK)
        phases = (places * order).astype(F32)
        size = count.astype(F32)
        phases = phases - jnp.floor(phases / size) * size
        angles = 2.0 * math.pi * phases / size
        cosine, sine = jnp.cos(angles), jnp.sin(angles)
        weights = jnp.where(order == 0, 1.0, 2.0) * jnp.where(2 * order < count, 1.0, 0.0)
        coarse_c = jnp.where(imaginary, -sine, cosine) * weights
        coarse_s = jnp.where(imaginary, cosine, sine) * weights
        for b in range(middle):
            turn_c, turn_s = cosine[tiny + b:tiny + b + 1], sine[tiny + b:tiny + b + 1]
            fcos_ref[pl.ds(b * tiny, tiny), :] = cosine[:tiny] * turn_c - sine[:tiny] * turn_s
            fsin_ref[pl.ds(b * tiny, tiny), :] = sine[:tiny] * turn_c + cosine[:tiny] * turn_s

        collect(2 * pair, 0)
        collect(2 * pair + 1, 1)
        even = held_ref[pl.ds(0, both_waves, stride=2), :]
        odd = held_ref[pl.ds(1, both_waves, stride=2), :]
        half = columns // 2
        basis = basis_ref[...]
        top = jnp.concatenate((basis, basis), axis=1)
        levels_both = jnp.concatenate((top, jnp.concatenate((basis, -basis), axis=1)), axis=0)
        real = jnp.concatenate((even[:, :half], odd[:, :half]), axis=1)
        imag = jnp.concatenate((even[:, half:], odd[:, half:]), axis=1)
        high, low = split(dot3(jnp.concatenate((real, imag), axis=0), levels_both))
        for b in range(points // BLOCK):
            lookup = coarse_c[first + b:first + b + 1] * fcos_ref[...] - coarse_s[first + b:first + b + 1] * fsin_ref[...]
            lookup_high, lookup_low = split(lookup)
            temps = dot(jnp.concatenate((lookup_high, lookup_low), axis=0), high)
            out_ref[pl.ds(b * BLOCK, BLOCK), :] += temps[:BLOCK] + temps[BLOCK:] + dot(lookup_high, low)

    lag = min(5, chunks)
    ahead = 2
    for owner in range(ahead):
        receive(owner)

    @pl.loop(0, chunks + lag + 1)
    def _(t):
        @pl.when(t + ahead < chunks)
        def _():
            receive(t + ahead)

        @pl.when(t < chunks)
        def _():
            compute(t)

        @pl.when(jnp.logical_and(t >= 1, t <= chunks))
        def _():
            merge_near(t - 1)

        @pl.when(jnp.logical_and(t >= lag, t < chunks + lag))
        def _():
            merge_side(t - lag)

        late = t - lag - 2

        @pl.when(jnp.logical_and(t >= lag + 2, late % 2 == 0))
        def _():
            finish(late // 2)

    for offset in others:
        target = other(offset)

        @pl.when(jnp.logical_and(sends, me + target < n))
        def _():
            leg_copy(me, target).wait_send()

    if paired:
        @pl.loop(0, n)
        def _(owner):
            @pl.when(jnp.logical_and(owner != me, jnp.logical_and(me + owner < n, owner % 2 == draw)))
            def _():
                pass_copy(owner).wait_send()

    @pl.loop(0, chunks)
    def _(q):
        @pl.when(q + 2 * chip < chunks)
        def _():
            near_copy(q).wait_send()
            side_copy(q).wait_send()

        @pl.when(q + 4 * layer < chunks)
        def _():
            for dz in range(1, layers):
                far_copy(q, layer, (layer + dz) % layers).wait_send()


def exchanged_sums(coefficients, legendre, row_counts, basis, n, draws, points):
    waves, _, slots, columns = coefficients.shape
    own, _, every, rows = legendre.shape
    dense = jnp.transpose(coefficients, (0, 2, 1, 3)).reshape(waves * slots * 2, columns)
    legs = jnp.transpose(legendre, (0, 1, 3, 2)).reshape(own * 2 * rows, every)
    layers, chunks = n // 4, n
    pairs = 128 // rows
    groups = own * 2 // pairs
    width = groups * pairs
    dma = pltpu.SemaphoreType.DMA

    def body(*refs):
        exchange_kernel(n, draws, waves, *refs)

    return pl.pallas_call(
        body,
        out_shape=jax.ShapeDtypeStruct((points, 2 * basis.shape[1]), F32),
        in_specs=[
            pl.BlockSpec(memory_space=pltpu.SMEM),
            pl.BlockSpec(memory_space=pl.ANY),
            pl.BlockSpec(memory_space=pltpu.VMEM),
            pl.BlockSpec(memory_space=pltpu.VMEM),
        ],
        out_specs=pl.BlockSpec(memory_space=pltpu.VMEM),
        scratch_shapes=[
            pltpu.VMEM(dense.shape, BF16),
            pltpu.VMEM((n, groups * slots, 128), F32),
            pltpu.VMEM((n, groups * slots, 128), F32),
            pltpu.VMEM((4 * slots, 128), F32),
            pltpu.VMEM((chunks, 2, 2, layers, width, columns), F32),
            pltpu.VMEM((chunks, 2, layers, width, columns), F32),
            pltpu.VMEM((chunks, layers, width, columns), F32),
            pltpu.VMEM((layers, chunks, width, columns), F32),
            pltpu.VMEM((2 * width, columns), F32),
            pltpu.VMEM((BLOCK, 4 * own), F32),
            pltpu.VMEM((BLOCK, 4 * own), F32),
            dma, dma((n,)), dma((n,)), dma((n,)),
            dma((chunks,)), dma((chunks,)),
            dma((chunks,)), dma((chunks,)),
            dma((layers, chunks)), dma((layers, chunks)),
        ],
        compiler_params=pltpu.CompilerParams(
            collective_id=0, has_side_effects=True, vmem_limit_bytes=58 * 1024 * 1024
        ),
        name="exchanged_sums",
    )(row_counts, dense, legs, basis)


def row_kernel(count_ref, temps_ref, absorb_ref, peak_ref, width_ref, out_ref, rhigh_ref, rlow_ref):
    step = pl.program_id(0)
    levels = absorb_ref.shape[1]
    points = temps_ref.shape[0]

    @pl.when(step == 0)
    def _():
        height = lax.broadcasted_iota(jnp.int32, rlow_ref.shape, 0)
        offsets = (height - peak_ref[...]).astype(F32) / width_ref[...]
        shape = jnp.exp(-offsets * offsets)
        high, low = split(shape / jnp.sum(shape, axis=0, keepdims=True))
        rhigh_ref[pl.ds(0, levels), :] = high
        rhigh_ref[pl.ds(levels, levels), :] = high
        rlow_ref[...] = low

    temps = jnp.concatenate((temps_ref[:, :levels], temps_ref[:, levels:]), axis=0)
    source = jnp.exp(0.5 * temps)
    layers = absorb_ref[...] * source
    before = lax.broadcasted_iota(jnp.int32, (2 * levels, levels), 0) % levels
    after = lax.broadcasted_iota(jnp.int32, (2 * levels, levels), 1)
    upper = jnp.where(before < after, 1.0, 0.0).astype(BF16)
    layers_high, layers_low = split(layers)
    above = dot(jnp.concatenate((layers_high, layers_low), axis=1), upper)
    emitted = source * jnp.exp(-above) * (1.0 - jnp.exp(-layers))
    place = step * points + lax.broadcasted_iota(jnp.int32, (2 * points, levels), 0) % points
    emitted = jnp.where(place < count_ref[0], emitted, 0.0)
    emitted_high, emitted_low = split(emitted)
    bright = dot(jnp.concatenate((emitted_high, emitted_low), axis=1), rhigh_ref[...])
    bright = bright + dot(emitted_high, rlow_ref[...])
    out_ref[0, 0] = bright[:points]
    out_ref[0, 1] = bright[points:]


def radiate_row(temps, row_counts, absorb, peak_level, width):
    points = temps.shape[0]
    levels, channels = absorb.shape[0], width.shape[0]

    def whole(*shape):
        return pl.BlockSpec(shape, lambda i, *_: (0,) * len(shape))

    return pl.pallas_call(
        row_kernel,
        out_shape=jax.ShapeDtypeStruct((1, 2, points, channels), F32),
        grid_spec=pltpu.PrefetchScalarGridSpec(
            num_scalar_prefetch=1,
            grid=(points // FINE,),
            in_specs=[
                pl.BlockSpec((FINE, 2 * levels), lambda i, *_: (i, 0)),
                whole(1, levels),
                whole(1, channels),
                whole(1, channels),
            ],
            out_specs=pl.BlockSpec((1, 2, FINE, channels), lambda i, *_: (0, 0, i, 0)),
            scratch_shapes=[
                pltpu.VMEM((2 * levels, channels), BF16),
                pltpu.VMEM((levels, channels), BF16),
            ],
        ),
        name="row_synthesis",
    )(row_counts, temps, absorb[None, :], peak_level[None, :], width[None, :])


def row_temperatures(spectra, row_count, basis, points):
    waves = spectra.shape[0] // 2
    orders = jnp.arange(waves, dtype=jnp.int32)
    places = jnp.arange(points, dtype=jnp.int32)
    phases = places[:, None] * orders[None, :] % row_count
    angles = 2.0 * math.pi * phases.astype(F32) / row_count.astype(F32)
    weights = jnp.where(orders == 0, 1.0, 2.0) * (2 * orders < row_count).astype(F32)
    parts = spectra.reshape(waves, 2, 2, basis.shape[0])
    fields = jnp.einsum("km,mpc->pkc", weights * jnp.cos(angles), parts[:, :, 0], precision=PRECISE)
    fields = fields - jnp.einsum("km,mpc->pkc", weights * jnp.sin(angles), parts[:, :, 1], precision=PRECISE)
    fields = jnp.einsum("pkc,cl->pkl", fields, basis, precision=PRECISE)
    return jnp.concatenate((fields[0] + fields[1], fields[0] - fields[1]), axis=1)


def moved_coefficients(coefficients, legendre):
    waves, _, slots, _ = coefficients.shape
    first = lax.axis_index("spec") * slots
    spread = prior_spread(jnp.arange(waves, dtype=jnp.int32), first + jnp.arange(slots, dtype=jnp.int32), waves)
    scaled = coefficients.astype(F32) * spread[..., None]
    spectral = lax.all_to_all(scaled, "spec", split_axis=0, concat_axis=2, tiled=True)
    sums = jnp.einsum("mpsj,mpsc->mpjc", legendre, spectral, precision=PRECISE)
    sums = lax.all_to_all(sums, "spec", split_axis=2, concat_axis=0, tiled=True)
    return sums.reshape(2 * waves, sums.shape[-1])


def on_device(draws, coefficients, legendre, row_counts, basis, absorb, peak_level, width):
    own, _, every, rows = legendre.shape
    waves, _, slots, columns = coefficients.shape
    n = waves // own
    fits = n == rows and n % 8 == 0 and 128 % n == 0 and every == n * slots and columns == 128
    fits = fits and (128 // n) % 8 == 0 and own % (128 // n) == 0 and slots % 4 == 0
    if fits and (slots * 128 // n) % 16 == 0 and 2 * waves >= 2 * slots * n:
        temps = exchanged_sums(coefficients, legendre, row_counts, basis, n, draws, NLON)
    else:
        temps = row_temperatures(moved_coefficients(coefficients, legendre), row_counts[0], basis, NLON)
    return radiate_row(temps, row_counts, absorb, peak_level, width)


def solution(mesh):
    placed = (
        P("draws", None, "spec", None),
        P("spec", None, None, None),
        P("spec"),
        P(),
        P(),
        P(),
        P(),
    )
    return jax.shard_map(
        functools.partial(on_device, mesh.shape["draws"]),
        mesh=mesh,
        in_specs=placed,
        out_specs=P(("draws", "spec"), None, None, None),
        check_vma=False,
    )
```

```python
import functools
import math

import jax
import jax.numpy as jnp
from jax import lax
from jax.experimental import pallas as pl
from jax.experimental.pallas import tpu as pltpu
from jax.sharding import PartitionSpec as P

NLON = 1280
FINE = 256

PRECISE = lax.Precision.HIGHEST
F32 = jnp.float32
BF16 = jnp.bfloat16


def prior_spread(orders, slots, waves):
    parity = jnp.arange(2, dtype=jnp.int32)[None, :, None]
    degree = orders[:, None, None] + 2 * slots[None, None, :] + parity
    spread = lax.rsqrt((degree + 1).astype(F32) * waves)
    return jnp.where(degree < waves, spread, jnp.zeros_like(spread))


def split(x):
    high = x.astype(BF16)
    return high, (x - high.astype(F32)).astype(BF16)


def dot(a, b):
    return jnp.dot(a, b, preferred_element_type=F32)


def dot3(a, b):
    ah, al = split(a)
    bh, bl = split(b)
    return dot(ah, bh) + dot(al, bh) + dot(ah, bl)


def place_in_ring(n):
    me = lax.axis_index("spec")
    core = me % 2
    side = (me // 2) % 2
    layer = me // 4
    return me, core, side, layer


def exchange_kernel(
    n, draws, waves, coef_hbm, leg_ref, out_ref, coef_ref, send_ref, legs_ref, wide_ref, sums_ref, near_ref, side_ref,
    far_ref, coef_sem, leg_send, leg_recv, pass_send, near_send, near_recv, side_send, side_recv, far_send, far_recv,
):
    me, core, side, layer = place_in_ring(n)
    layers = n // 4
    chunks = n
    chip = me // 2
    draw = lax.axis_index("draws")
    rows = n
    columns = coef_hbm.shape[1]
    every = leg_ref.shape[1]
    slots = every // n
    lanes = 128
    pairs = lanes // rows
    per = pairs // 2
    own = waves // n
    groups = own // per
    depth = per * slots * 2
    part = groups * pairs
    partner = me + 1 - 2 * core
    across = me + 2 - 4 * side

    def spot(z, y, c):
        return (z * 2 + y) * 2 + c

    def remote(src, dst, send_sem, recv_sem, target):
        return pltpu.make_async_remote_copy(
            src_ref=src, dst_ref=dst, send_sem=send_sem, recv_sem=recv_sem,
            device_id={"spec": target}, device_id_type=pl.DeviceIdType.MESH,
        )

    def leg_copy(source, target):
        return remote(send_ref.at[target], legs_ref.at[source], leg_send.at[target], leg_recv.at[source], target)

    def pass_copy(source):
        return pltpu.make_async_remote_copy(
            src_ref=legs_ref.at[source], dst_ref=legs_ref.at[source],
            send_sem=pass_send.at[source], recv_sem=leg_recv.at[source],
            device_id={"draws": 1 - draw}, device_id_type=pl.DeviceIdType.MESH,
        )

    def near_copy(q):
        return remote(sums_ref.at[q, 1 - core], near_ref.at[q], near_send.at[q], near_recv.at[q], partner)

    def side_copy(q):
        return remote(sums_ref.at[q, core, 1 - side], side_ref.at[q], side_send.at[q], side_recv.at[q], across)

    def far_copy(q, source, target):
        return remote(
            sums_ref.at[q, core, side, target], far_ref.at[source, q],
            far_send.at[target, q], far_recv.at[source, q], spot(target, side, core),
        )

    others = [(dz, dy, dc) for dz in range(layers) for dy in range(2) for dc in range(2)][1:]

    def other(offset):
        dz, dy, dc = offset
        return spot((layer + dz) % layers, (side + dy) % 2, (core + dc) % 2)

    coef_copy = pltpu.make_async_copy(coef_hbm, coef_ref, coef_sem)
    coef_copy.start()
    paired = draws == 2
    barrier = pltpu.get_barrier_semaphore()
    if paired:
        pl.semaphore_signal(barrier, inc=1, device_id={"draws": 1 - draw}, device_id_type=pl.DeviceIdType.MESH)
    for offset in others:
        pl.semaphore_signal(barrier, inc=1, device_id={"spec": other(offset)}, device_id_type=pl.DeviceIdType.MESH)

    row = lax.broadcasted_iota(jnp.int32, (lanes, lanes), 0)
    lane = lax.broadcasted_iota(jnp.int32, (lanes, lanes), 1)
    row_at = row % rows
    ordered = ((row_at % 2) * 2 + (row_at // 2) % 2) * layers + row_at // 4
    moves = jnp.where(ordered * pairs + row // rows == lane, 1.0, 0.0)
    leg_row = lax.broadcasted_iota(jnp.int32, (lanes, every), 0) // rows
    leg_slot = lax.broadcasted_iota(jnp.int32, (lanes, every), 1)
    degree_part = leg_row // 2 + leg_row % 2 + 2 * leg_slot

    @pl.loop(0, groups // 2)
    def _(double):
        turned = []
        for half in range(2):
            g = double * 2 + half
            degree = degree_part + (me * own + g * per)
            spread = lax.rsqrt((degree + 1).astype(F32) * float(waves))
            spread = jnp.where(degree < waves, spread, 0.0)
            values = leg_ref[pl.ds(pl.multiple_of(g * lanes, lanes), lanes), :] * spread
            turned.append(
                lax.dot_general(
                    values, moves, (((0,), (0,)), ((), ())), precision=PRECISE, preferred_element_type=F32
                )
            )
        for k in range(n):
            piece = [t[k * slots:(k + 1) * slots] for t in turned]
            send_ref[k, pl.ds(pl.multiple_of(double * 2 * slots, 2 * slots), 2 * slots), :] = jnp.concatenate(piece, 0)

    pl.semaphore_wait(barrier, len(others) + paired)
    sends = (core == draw) if paired else (core >= 0)
    for offset in others:
        target = other(offset)

        @pl.when(jnp.logical_and(sends, me + target < n))
        def _():
            leg_copy(me, target).start()

    legs_ref[me] = send_ref[me]
    coef_copy.wait()

    def receive(owner):
        wanted = jnp.logical_and(owner != me, me + owner < n)
        if not paired:
            return

        @pl.when(jnp.logical_and(wanted, owner % 2 == draw))
        def _():
            leg_copy(owner, me).wait_recv()
            pass_copy(owner).start()

    expand_row = lax.broadcasted_iota(jnp.int32, (depth, lanes), 0)
    expand_lane = lax.broadcasted_iota(jnp.int32, (depth, lanes), 1) % pairs
    keep = (expand_row // (2 * slots)) * 2 + expand_row % 2 == expand_lane

    def partial(q):
        owner = q

        @pl.when(me + owner < n)
        def _():
            waits = owner != me
            if paired:
                waits = jnp.logical_and(waits, owner % 2 != draw)

            @pl.when(waits)
            def _():
                leg_copy(owner, me).wait_recv()

            @pl.loop(0, groups // 2)
            def _(double):
                legs = legs_ref[owner, pl.ds(pl.multiple_of(double * 2 * slots, 2 * slots), 2 * slots), :]
                wide_ref[pl.ds(0, 2 * slots, stride=2), :] = legs
                wide_ref[pl.ds(1, 2 * slots, stride=2), :] = legs
                for half in range(2):
                    g = owner * groups + double * 2 + half
                    values = coef_ref[pl.ds(pl.multiple_of(g * depth, depth), depth), :]
                    one = wide_ref[pl.ds(half * 2 * slots, 2 * slots), :]
                    tiled = jnp.where(keep, jnp.concatenate([one] * per, axis=0), 0.0)
                    both = jnp.concatenate(split(tiled), axis=1)
                    sums = lax.dot_general(both, values, (((0,), (0,)), ((), ())), preferred_element_type=F32)
                    sums = (sums[:lanes] + sums[lanes:]).reshape(2, 2, layers, pairs, columns)
                    at = pl.multiple_of((double * 2 + half) * pairs, pairs)
                    sums_ref[q, :, :, :, pl.ds(at, pairs), :] = sums

        @pl.when(me + owner >= n)
        def _():
            sums_ref[q] = jnp.zeros((2, 2, layers, part, columns), F32)

    def compute(q):
        @pl.when(q + 2 * chip < chunks)
        def _():
            partial(q)
            near_copy(q).start()

    def merge_near(q):
        @pl.when(q + 2 * chip < chunks)
        def _():
            near_copy(q).wait_recv()

            for y in (0, 1):
                @pl.loop(0, layers)
                def _(z):
                    sums_ref[q, core, y, z] += near_ref[q, y, z]

            side_copy(q).start()

    def merge_side(q):
        here = q + 2 * chip < chunks
        there = q + 2 * (across // 2) < chunks

        @pl.when(there)
        def _():
            side_copy(q).wait_recv()

        @pl.when(jnp.logical_and(here, there))
        def _():
            @pl.loop(0, layers)
            def _(z):
                sums_ref[q, core, side, z] += side_ref[q, z]

        @pl.when(jnp.logical_and(jnp.logical_not(here), there))
        def _():
            @pl.loop(0, layers)
            def _(z):
                sums_ref[q, core, side, z] = side_ref[q, z]

        @pl.when(jnp.logical_or(here, there))
        def _():
            for dz in range(1, layers):
                far_copy(q, layer, (layer + dz) % layers).start()

    lag = min(5, chunks)
    ahead = 2
    for owner in range(ahead):
        receive(owner)

    @pl.loop(0, chunks + 1)
    def _(t):
        @pl.when(t + ahead < chunks)
        def _():
            receive(t + ahead)

        @pl.when(t < chunks)
        def _():
            compute(t)

        @pl.when(t >= 1)
        def _():
            merge_near(t - 1)

        @pl.when(t >= lag)
        def _():
            merge_side(t - lag)

    @pl.loop(chunks + 1 - lag, chunks)
    def _(q):
        merge_side(q)

    @pl.loop(0, chunks)
    def _(q):
        at = pl.ds(pl.multiple_of(q * part, part), part)

        @pl.when(q + 4 * layer < chunks)
        def _():
            out_ref[at, :] = sums_ref[q, core, side, layer]

        @pl.when(q + 4 * layer >= chunks)
        def _():
            out_ref[at, :] = jnp.zeros((part, columns), F32)

        for dz in range(1, layers):
            source = (layer + dz) % layers

            @pl.when(q + 4 * source < chunks)
            def _():
                far_copy(q, source, layer).wait_recv()
                out_ref[at, :] += far_ref[source, q]

    for offset in others:
        target = other(offset)

        @pl.when(jnp.logical_and(sends, me + target < n))
        def _():
            leg_copy(me, target).wait_send()

    if paired:
        @pl.loop(0, n)
        def _(owner):
            @pl.when(jnp.logical_and(owner != me, jnp.logical_and(me + owner < n, owner % 2 == draw)))
            def _():
                pass_copy(owner).wait_send()

    @pl.loop(0, chunks)
    def _(q):
        @pl.when(q + 2 * chip < chunks)
        def _():
            near_copy(q).wait_send()
            side_copy(q).wait_send()

        @pl.when(q + 4 * layer < chunks)
        def _():
            for dz in range(1, layers):
                far_copy(q, layer, (layer + dz) % layers).wait_send()


def exchanged_sums(coefficients, legendre, n, draws):
    waves, _, slots, columns = coefficients.shape
    own, _, every, rows = legendre.shape
    dense = jnp.transpose(coefficients, (0, 2, 1, 3)).reshape(waves * slots * 2, columns)
    legs = jnp.transpose(legendre, (0, 1, 3, 2)).reshape(own * 2 * rows, every)
    layers, chunks = n // 4, n
    pairs = 128 // rows
    groups = own * 2 // pairs
    width = groups * pairs
    dma = pltpu.SemaphoreType.DMA

    def body(*refs):
        exchange_kernel(n, draws, waves, *refs)

    return pl.pallas_call(
        body,
        out_shape=jax.ShapeDtypeStruct((2 * waves, columns), F32),
        in_specs=[pl.BlockSpec(memory_space=pl.ANY), pl.BlockSpec(memory_space=pltpu.VMEM)],
        out_specs=pl.BlockSpec(memory_space=pltpu.VMEM),
        scratch_shapes=[
            pltpu.VMEM(dense.shape, BF16),
            pltpu.VMEM((n, groups * slots, 128), F32),
            pltpu.VMEM((n, groups * slots, 128), F32),
            pltpu.VMEM((4 * slots, 128), F32),
            pltpu.VMEM((chunks, 2, 2, layers, width, columns), F32),
            pltpu.VMEM((chunks, 2, layers, width, columns), F32),
            pltpu.VMEM((chunks, layers, width, columns), F32),
            pltpu.VMEM((layers, chunks, width, columns), F32),
            dma, dma((n,)), dma((n,)), dma((n,)),
            dma((chunks,)), dma((chunks,)),
            dma((chunks,)), dma((chunks,)),
            dma((layers, chunks)), dma((layers, chunks)),
        ],
        compiler_params=pltpu.CompilerParams(
            collective_id=0, has_side_effects=True, vmem_limit_bytes=58 * 1024 * 1024
        ),
        name="exchanged_sums",
    )(dense, legs)


def row_kernel(
    count_ref, spectra_ref, basis_ref, absorb_ref, peak_ref, width_ref, out_ref,
    fcos_ref, fsin_ref, ccos_ref, csin_ref, high_ref, low_ref, rhigh_ref, rlow_ref,
):
    step = pl.program_id(0)
    waves = fcos_ref.shape[1]
    levels = absorb_ref.shape[1]
    points = fcos_ref.shape[0]
    tiny = 16
    middle = points // tiny

    @pl.when(step == 0)
    def _():
        count = count_ref[0].astype(F32)
        table = (tiny + middle + ccos_ref.shape[0], waves)
        index = lax.broadcasted_iota(jnp.int32, table, 0)
        order = lax.broadcasted_iota(jnp.int32, table, 1)
        places = jnp.where(index < tiny, index, (index - tiny) * tiny)
        places = jnp.where(index < tiny + middle, places, (index - tiny - middle) * points)
        phases = (places * order).astype(F32)
        phases = phases - jnp.floor(phases / count) * count
        angles = 2.0 * math.pi * phases / count
        cosine, sine = jnp.cos(angles), jnp.sin(angles)
        weights = jnp.where(order == 0, 1.0, 2.0) * jnp.where(2 * order < count_ref[0], 1.0, 0.0)
        first = tiny + middle
        ccos_ref[...] = (cosine * weights)[first:]
        csin_ref[...] = (sine * weights)[first:]
        for b in range(middle):
            turn_c, turn_s = cosine[tiny + b:tiny + b + 1], sine[tiny + b:tiny + b + 1]
            fcos_ref[pl.ds(b * tiny, tiny), :] = cosine[:tiny] * turn_c - sine[:tiny] * turn_s
            fsin_ref[pl.ds(b * tiny, tiny), :] = sine[:tiny] * turn_c + cosine[:tiny] * turn_s

        even = spectra_ref[pl.ds(0, waves, stride=2), :]
        odd = spectra_ref[pl.ds(1, waves, stride=2), :]
        half = even.shape[1] // 2
        real = jnp.concatenate((even[:, :half], odd[:, :half]), axis=1)
        imag = jnp.concatenate((even[:, half:], odd[:, half:]), axis=1)
        basis = basis_ref[...]
        top = jnp.concatenate((basis, basis), axis=1)
        wide = jnp.concatenate((top, jnp.concatenate((basis, -basis), axis=1)), axis=0)
        for index, piece in enumerate((real, imag)):
            high, low = split(dot3(piece, wide))
            high_ref[pl.ds(index * waves, waves), :] = high
            low_ref[pl.ds(index * waves, waves), :] = low
        height = lax.broadcasted_iota(jnp.int32, rlow_ref.shape, 0)
        offsets = (height - peak_ref[...]).astype(F32) / width_ref[...]
        shape = jnp.exp(-offsets * offsets)
        high, low = split(shape / jnp.sum(shape, axis=0, keepdims=True))
        rhigh_ref[pl.ds(0, levels), :] = high
        rhigh_ref[pl.ds(levels, levels), :] = high
        rlow_ref[...] = low

    base_c = ccos_ref[pl.ds(step, 1), :]
    base_s = csin_ref[pl.ds(step, 1), :]
    fine_c = fcos_ref[...]
    fine_s = fsin_ref[...]
    cosine = base_c * fine_c - base_s * fine_s
    sine = -(base_s * fine_c + base_c * fine_s)
    lookup_high, lookup_low = split(jnp.concatenate((cosine, sine), axis=1))
    temps = dot(jnp.concatenate((lookup_high, lookup_low), axis=0), high_ref[...])
    temps = temps[:points] + temps[points:] + dot(lookup_high, low_ref[...])
    temps = jnp.concatenate((temps[:, :levels], temps[:, levels:]), axis=0)

    source = jnp.exp(0.5 * temps)
    layers = absorb_ref[...] * source
    before = lax.broadcasted_iota(jnp.int32, (2 * levels, levels), 0) % levels
    after = lax.broadcasted_iota(jnp.int32, (2 * levels, levels), 1)
    upper = jnp.where(before < after, 1.0, 0.0).astype(BF16)
    layers_high, layers_low = split(layers)
    above = dot(jnp.concatenate((layers_high, layers_low), axis=1), upper)
    emitted = source * jnp.exp(-above) * (1.0 - jnp.exp(-layers))
    place = step * points + lax.broadcasted_iota(jnp.int32, (2 * points, levels), 0) % points
    emitted = jnp.where(place < count_ref[0], emitted, 0.0)
    emitted_high, emitted_low = split(emitted)
    bright = dot(jnp.concatenate((emitted_high, emitted_low), axis=1), rhigh_ref[...])
    bright = bright + dot(emitted_high, rlow_ref[...])
    out_ref[0, 0] = bright[:points]
    out_ref[0, 1] = bright[points:]


def synthesize_row(spectra, row_counts, basis, absorb, peak_level, width, points):
    waves = spectra.shape[0] // 2
    levels, channels = absorb.shape[0], width.shape[0]
    columns = spectra.shape[1]
    steps = points // FINE
    coarse = -(-steps // 8) * 8

    def whole(*shape):
        return pl.BlockSpec(shape, lambda i, *_: (0,) * len(shape))

    return pl.pallas_call(
        row_kernel,
        out_shape=jax.ShapeDtypeStruct((1, 2, points, channels), F32),
        grid_spec=pltpu.PrefetchScalarGridSpec(
            num_scalar_prefetch=1,
            grid=(steps,),
            in_specs=[
                whole(2 * waves, columns),
                whole(*basis.shape),
                whole(1, levels),
                whole(1, channels),
                whole(1, channels),
            ],
            out_specs=pl.BlockSpec((1, 2, FINE, channels), lambda i, *_: (0, 0, i, 0)),
            scratch_shapes=[
                pltpu.VMEM((FINE, waves), F32),
                pltpu.VMEM((FINE, waves), F32),
                pltpu.VMEM((coarse, waves), F32),
                pltpu.VMEM((coarse, waves), F32),
                pltpu.VMEM((2 * waves, 2 * levels), BF16),
                pltpu.VMEM((2 * waves, 2 * levels), BF16),
                pltpu.VMEM((2 * levels, channels), BF16),
                pltpu.VMEM((levels, channels), BF16),
            ],
        ),
        name="row_synthesis",
    )(row_counts, spectra, basis, absorb[None, :], peak_level[None, :], width[None, :])


def moved_coefficients(coefficients, legendre):
    waves, _, slots, _ = coefficients.shape
    first = lax.axis_index("spec") * slots
    spread = prior_spread(jnp.arange(waves, dtype=jnp.int32), first + jnp.arange(slots, dtype=jnp.int32), waves)
    scaled = coefficients.astype(F32) * spread[..., None]
    spectral = lax.all_to_all(scaled, "spec", split_axis=0, concat_axis=2, tiled=True)
    sums = jnp.einsum("mpsj,mpsc->mpjc", legendre, spectral, precision=PRECISE)
    sums = lax.all_to_all(sums, "spec", split_axis=2, concat_axis=0, tiled=True)
    return sums.reshape(2 * waves, sums.shape[-1])


def on_device(draws, coefficients, legendre, row_counts, basis, absorb, peak_level, width):
    own, _, every, rows = legendre.shape
    waves, _, slots, columns = coefficients.shape
    n = waves // own
    fits = n == rows and n % 8 == 0 and 128 % n == 0 and every == n * slots and columns == 128
    fits = fits and (128 // n) % 8 == 0 and own % (128 // n) == 0 and slots % 4 == 0
    if fits and (slots * 128 // n) % 16 == 0 and 2 * waves >= 2 * slots * n:
        spectra = exchanged_sums(coefficients, legendre, n, draws)
    else:
        spectra = moved_coefficients(coefficients, legendre)
    return synthesize_row(spectra, row_counts, basis, absorb, peak_level, width, NLON)


def solution(mesh):
    placed = (
        P("draws", None, "spec", None),
        P("spec", None, None, None),
        P("spec"),
        P(),
        P(),
        P(),
        P(),
    )
    return jax.shard_map(
        functools.partial(on_device, mesh.shape["draws"]),
        mesh=mesh,
        in_specs=placed,
        out_specs=P(("draws", "spec"), None, None, None),
        check_vma=False,
    )
```
